256 devices in a mesh: dp: 4 (over y), outer: 4 (over x_hi, core), inner: 16 (over z, x_lo).
Axes of the slice: x: 4 (x_hi: 2, x_lo: 2; x = x_hi * 2 + x_lo), y: 4, z: 8, core: 2. Of those that a mesh axis runs over, the one named last changes fastest.
Arguments:
- activations: bfloat16 [4, 8192, 4096], P('dp', ('outer', 'inner')), may hold values from -28 to 28
- weights: bfloat16 [4096, 384], P('dp'), may hold values from -0.09375 to 0.09375
- positions: int32 [4, 8192], P('dp', ('outer', 'inner')), may hold values from 0 to 8191, each once within a row
- out_grad: bfloat16 [4, 8192, 128], P('dp', ('outer', 'inner')), may hold values from -6 to 6
Outputs:
- grad_activations: float32 [4, 8192, 4096], P('dp', ('outer', 'inner'))
- grad_weights: float32 [4096, 384], P('dp')
The draws below stay inside these ranges and needn't reach their ends.
Inputs may be any that keep to these rules, and one draw needn't show every extreme that they name: Each row of positions holds every position of its sequence once.
All inputs are finite; a program needn't handle non-finite values.
Results may differ from the reference program's by a relative error of at most 0.024.
Values may be sent and summed in bfloat16 or wider, within the bound.
A program may use at most 64 MiB of HBM per device.

```python
import jax
import jax.numpy as jnp
from jax import lax

D = 4096
HEADS = 1
HEAD_DIM = 128
SEQ = 8192
BATCH = 4


def draw_activations(key, part):
    base_key = jax.random.fold_in(key, 0)
    return jnp.clip(jax.random.normal(base_key, (BATCH, SEQ, D), jnp.float32), -6.0, 6.0).astype(jnp.bfloat16)


def level_of(own_key, extent, shards, low, high):
    def one(dim, parts):
        heights = jax.random.uniform(jax.random.fold_in(jax.random.fold_in(own_key, 6), dim), (parts,), jnp.float32, low / len(shards), high / len(shards))
        return jnp.repeat(jnp.exp(heights), extent[dim] // parts).reshape((-1,) + (1,) * (len(extent) - dim - 1))

    gain = one(*shards[0])
    for cut in shards[1:]:
        gain = gain * one(*cut)
    return gain


def normal_values(stream_key, dims, scale, most, pieces=(), held_as=jnp.bfloat16):
    factor_of = level_of(stream_key, dims, pieces, -0.22, 0.18) if pieces else 1.0
    values = jax.random.normal(stream_key, dims, jnp.float32) * scale * factor_of
    return jnp.minimum(jnp.maximum(values, -most), most).astype(held_as)


def setup_inputs(seed: int = 0) -> dict:
    streams_of = jax.random.split(jax.random.key(seed), 5)
    activations = draw_activations(jax.random.fold_in(streams_of[4], 71), 0)
    weights = normal_values(streams_of[1], (D, (HEADS + 2) * HEAD_DIM), D ** -0.5, 0.09375, ((0, 4),))
    positions = jax.vmap(lambda own: jax.random.permutation(own, SEQ))(jax.random.split(streams_of[2], BATCH)).reshape((BATCH, SEQ)).astype(jnp.int32)
    out_grad = normal_values(streams_of[3], (BATCH, SEQ, HEADS * HEAD_DIM), 1.0, 6.0, ((0, 4), (1, 64)))
    return dict(activations=activations, weights=weights, positions=positions, out_grad=out_grad)


ROPE_BASE = 500000.0
HIGH = lax.Precision.HIGHEST


def rope_tables(places):
    half_dim = HEAD_DIM // 2
    steps_up = jnp.arange(half_dim, dtype=jnp.float32)
    frequency = ROPE_BASE ** (-(steps_up * 2.0 / HEAD_DIM))
    angles = places.astype(jnp.float32)[:, None] * frequency[None, :]
    cosine_rows = jnp.cos(angles)
    sine_rows = jnp.sin(angles)
    return jnp.concatenate([cosine_rows, cosine_rows], 1), jnp.concatenate([sine_rows, sine_rows], 1)


def rotate(values, cosine_rows, sine_rows, direction):
    half_dim = values.shape[-1] // 2
    turned = jnp.concatenate([-values[..., half_dim:], values[..., :half_dim]], -1)
    return values * cosine_rows + direction * turned * sine_rows


def group_grads(local_activations, places, out_rows, weights):
    seq_len = local_activations.shape[0]
    width_q = HEADS * HEAD_DIM
    score_scale = HEAD_DIM ** -0.5
    projected = jnp.dot(local_activations, weights, preferred_element_type=jnp.float32)
    cosine_rows, sine_rows = rope_tables(places)
    queries = projected[:, :width_q].reshape(seq_len, HEADS, HEAD_DIM).transpose(1, 0, 2)
    queries = rotate(queries, cosine_rows, sine_rows, 1.0).astype(jnp.bfloat16)
    keys_all = rotate(projected[:, width_q:width_q + HEAD_DIM], cosine_rows, sine_rows, 1.0).astype(jnp.bfloat16)
    values_all = projected[:, width_q + HEAD_DIM:].astype(jnp.bfloat16)
    grad_heads = out_rows.reshape(seq_len, HEADS, HEAD_DIM).transpose(1, 0, 2)
    keys_wide = keys_all.astype(jnp.float32)
    values_wide = values_all.astype(jnp.float32)
    block_rows = min(512, seq_len)
    block_count = seq_len // block_rows

    def one_block(running, block_index):
        grad_key, grad_value = running
        offset = block_index * block_rows
        query_block = lax.dynamic_slice_in_dim(queries, offset, block_rows, 1).astype(jnp.float32)
        place_block = lax.dynamic_slice_in_dim(places, offset, block_rows, 0)
        grad_block = lax.dynamic_slice_in_dim(grad_heads, offset, block_rows, 1).astype(jnp.float32)
        scores = jnp.einsum('hqd,kd->hqk', query_block, keys_wide, precision=HIGH) * score_scale
        visible = place_block[:, None] >= places[None, :]
        scores = jnp.where(visible[None], scores, -jnp.inf)
        attn_probs = jax.nn.softmax(scores, axis=-1)
        rounded = attn_probs.astype(jnp.bfloat16).astype(jnp.float32)
        outputs = jnp.einsum('hqk,kd->hqd', attn_probs, values_wide, precision=HIGH)
        delta_rows = jnp.sum(grad_block * outputs, -1)
        grad_value = grad_value + jnp.einsum('hqk,hqd->kd', rounded, grad_block, precision=HIGH)
        grad_probs = jnp.einsum('hqd,kd->hqk', grad_block, values_wide, precision=HIGH)
        grad_scores = (attn_probs * (grad_probs - delta_rows[..., None])).astype(jnp.bfloat16).astype(jnp.float32)
        grad_query = jnp.einsum('hqk,kd->hqd', grad_scores, keys_wide, precision=HIGH) * score_scale
        grad_key = grad_key + jnp.einsum('hqk,hqd->kd', grad_scores, query_block, precision=HIGH) * score_scale
        return (grad_key, grad_value), grad_query

    zero_rows = jnp.zeros((seq_len, HEAD_DIM), jnp.float32)
    sums, grad_query = lax.scan(one_block, (zero_rows, zero_rows), jnp.arange(block_count, dtype=jnp.int32))
    grad_key, grad_value = sums
    grad_query = grad_query.transpose(1, 0, 2, 3).reshape(HEADS, seq_len, HEAD_DIM)
    grad_query = rotate(grad_query, cosine_rows, sine_rows, -1.0)
    grad_key = rotate(grad_key, cosine_rows, sine_rows, -1.0)
    grad_proj = jnp.concatenate([grad_query.transpose(1, 0, 2).reshape(seq_len, width_q), grad_key, grad_value], 1).astype(jnp.bfloat16)
    grad_acts = lax.dot_general(grad_proj, weights, (((1,), (1,)), ((), ())), preferred_element_type=jnp.float32)
    grad_weight = lax.dot_general(local_activations, grad_proj, (((0,), (0,)), ((), ())), preferred_element_type=jnp.float32)
    return grad_acts, grad_weight


def reference(activations, weights, positions, out_grad):
    def per_group(group_index):
        return group_grads(activations[group_index], positions[group_index], out_grad[group_index], weights)

    grad_acts, grad_parts = lax.map(per_group, jnp.arange(BATCH, dtype=jnp.int32))
    return grad_acts, jnp.sum(grad_parts, 0)
```

```python
import jax
import jax.numpy as jnp
import numpy as np
from jax import lax
from jax.experimental import pallas as pl
from jax.experimental.pallas import tpu as pltpu
from jax.sharding import PartitionSpec as P

HEAD_DIM = 128
ROPE_BASE = 500000.0
NX, NY, NZ, NC = 4, 4, 8, 2
TOK = 128
WIDE = 3 * HEAD_DIM
MESH = pl.DeviceIdType.MESH
BF = jnp.bfloat16
F32 = jnp.float32
SCALE = HEAD_DIM ** (-0.5)
EXP2_SCALE = SCALE * 1.4426950408889634
LOW = -1e30


def coords():
    outer, inner = lax.axis_index("outer"), lax.axis_index("inner")
    return (
        (outer // 2) * 2 + lax.rem(inner, 2),
        lax.axis_index("dp"),
        inner // 2,
        lax.rem(outer, 2),
    )


def device(x, y, z, c):
    return {"dp": y, "outer": (x // 2) * 2 + c, "inner": z * 2 + lax.rem(x, 2)}


def nt(a, b):
    return lax.dot_general(a, b, (((1,), (1,)), ((), ())), preferred_element_type=F32)


def nn(a, b):
    return lax.dot_general(a, b, (((1,), (0,)), ((), ())), preferred_element_type=F32)


def turn(u):
    lane = lax.broadcasted_iota(jnp.int32, u.shape, 1)
    half = jnp.roll(u, HEAD_DIM // 2, 1) if False else pltpu.roll(u, HEAD_DIM // 2, 1)
    return jnp.where(lane < HEAD_DIM // 2, -half, half)


def kernel(
    freq_ref, act_hbm, w_hbm, pos_hbm, og_hbm, ga_hbm, gw_hbm,
    act_v, w_v, og_all, q_all, posq, posk, poskt, kv_all, kt_all, proj,
    e_all, dp_all, ds_all, mb, lb, ab, st_all,
    dq_out, dq_in, dkv_out, dkv_in, gp_all, actx, actxt,
    dwx_out, dwx_in, dwx_own, dwz_out, dwz_in, dw_all, ga_v, gw_v,
    lsem, wsem_s, wsem_r, osem_s, osem_r, psem_s, psem_r, ksem_s, ksem_r,
    qsem_s, qsem_r, kvsem_s, kvsem_r, asem_s, asem_r, ssem_s, ssem_r,
    dqsem_s, dqsem_r, dkvsem_s, dkvsem_r, gsem_s, gsem_r,
    xsem_s, xsem_r, zsem_s, zsem_r, zgsem_s, zgsem_r, xgsem_s, xgsem_r,
):
    x, y, z, c = coords()
    other = 1 - c
    xc, yc = x * 2 + c, y * 2 + c
    sends = []

    def xpeer(k):
        return device(lax.rem(x + k, NX), y, z, c)

    def ypeer(k):
        return device(x, lax.rem(y + k, NY), z, c)

    def zpeer(k):
        return device(x, y, lax.rem(z + k, NZ), c)

    sibling = device(x, y, z, other)

    def send(src, dst, ss, rs, dev):
        cp = pltpu.make_async_remote_copy(src, dst, ss, rs, device_id=dev, device_id_type=MESH)
        cp.start()
        sends.append(cp)

    def arrived(dst, rs):
        pltpu.make_async_remote_copy(
            dst, dst, rs, rs, device_id=sibling, device_id_type=MESH
        ).wait_recv()

    def rows(i, n):
        return pl.ds(pl.multiple_of(i * n, n), n)

    cross = [(k, d) for k in range(4) for d in range(2)][1:]

    lw = pltpu.make_async_copy(w_hbm, w_v.at[rows(y, 1024)], lsem.at[0])
    lw.start()
    lp = pltpu.make_async_copy(pos_hbm, posq.at[z], lsem.at[1])
    lp.start()
    lo = pltpu.make_async_copy(og_hbm.at[0], og_all.at[rows(z, TOK)], lsem.at[2])
    lo.start()
    la = pltpu.make_async_copy(act_hbm.at[0], act_v, lsem.at[3])
    la.start()
    lk = pltpu.make_async_copy(pos_hbm, posk.at[xc], lsem.at[4])
    lk.start()

    barrier = pltpu.get_barrier_semaphore()
    greet = [sibling] + [zpeer(k) for k in range(1, NZ)]
    for k in range(1, 4):
        greet += [xpeer(k), ypeer(k)]
        greet += [
            device(lax.rem(x + k, NX), y, z, other),
            device(x, lax.rem(y + k, NY), z, other),
        ]
    for dev in greet:
        pl.semaphore_signal(barrier, inc=1, device_id=dev, device_id_type=MESH)
    pl.semaphore_wait(barrier, len(greet))

    KVC, QC = pl.ds(HEAD_DIM, 2 * HEAD_DIM), pl.ds(0, HEAD_DIM)

    def wblock(owner, half, cols):
        return w_v.at[pl.ds(pl.multiple_of(owner * 1024 + half * 512, 512), 512), cols]

    lw.wait()
    YORDER = (1, 3, 2)
    for part, cols in enumerate((KVC, QC)):
        for k in YORDER:
            blk = wblock(y, c, cols)
            send(blk, blk, wsem_s.at[part, 0, k], wsem_r.at[part, 0, k], ypeer(k))
    lo.wait()
    lp.wait()
    lk.wait()
    for k in range(1, NZ):
        blk = posq.at[z]
        send(blk, blk, psem_s.at[k], psem_r.at[k], zpeer(k))
    for k, d in cross:
        blk = posk.at[xc]
        dev = device(lax.rem(x + k, NX), y, z, c if d == 0 else other)
        send(blk, blk, ksem_s.at[2 * k + d], ksem_r.at[2 * k + d], dev)
    for k in range(1, NZ):
        blk = og_all.at[rows(z, TOK)]
        send(blk, blk, osem_s.at[k], osem_r.at[k], zpeer(k))

    place = posq[z].astype(F32)
    angles = jnp.broadcast_to(place, (TOK, HEAD_DIM)).T * freq_ref[...]
    cosine, sine = jnp.cos(angles), jnp.sin(angles)

    la.wait()

    def acts(owner):
        return act_v[:, pl.ds(pl.multiple_of(owner * 1024, 1024), 1024)]

    proj[...] = nn(acts(y), w_v[rows(y, 1024), :])
    for part, cols in enumerate((KVC, QC)):
        for k in YORDER:
            owner = lax.rem(y - k + NY, NY)
            blk = wblock(owner, c, cols)
            arrived(blk, wsem_r.at[part, 0, k])
            send(blk, blk, wsem_s.at[part, 1, k], wsem_r.at[part, 1, k], sibling)
        for k in YORDER:
            owner = lax.rem(y - k + NY, NY)
            arrived(wblock(owner, other, cols), wsem_r.at[part, 1, k])
            proj[:, cols] += nn(acts(owner), w_v[rows(owner, 1024), cols])
        if part == 0:
            keys = proj[:, HEAD_DIM : 2 * HEAD_DIM]
            keys = keys * cosine + turn(keys) * sine
            kv_all[xc, :, :HEAD_DIM] = keys.astype(BF)
            kv_all[xc, :, HEAD_DIM:] = proj[:, 2 * HEAD_DIM :].astype(BF)
            for k, d in cross:
                blk = kv_all.at[xc]
                dev = device(lax.rem(x + k, NX), y, z, c if d == 0 else other)
                send(blk, blk, kvsem_s.at[2 * k + d], kvsem_r.at[2 * k + d], dev)
    queries = proj[:, :HEAD_DIM]
    queries = queries * cosine + turn(queries) * sine
    q_all[rows(z, TOK), :] = queries.astype(BF)
    for k in range(1, NZ):
        blk = q_all.at[rows(z, TOK)]
        send(blk, blk, qsem_s.at[k], qsem_r.at[k], zpeer(k))

    for k, d in cross:
        to_y, to_c = lax.rem(y + k, NY), c if d == 0 else other
        src = act_v.at[:, pl.ds(pl.multiple_of(to_y * 1024 + to_c * 512, 512), 512)]
        send(src, actx.at[yc], asem_s.at[2 * k + d], asem_r.at[2 * k + d], device(x, to_y, z, to_c))
    lx = pltpu.make_async_copy(
        act_v.at[:, pl.ds(pl.multiple_of(y * 1024 + c * 512, 512), 512)], actx.at[yc], lsem.at[5]
    )
    lx.start()

    for k in range(1, NZ):
        arrived(posq.at[lax.rem(z - k + NZ, NZ)], psem_r.at[k])
    for k, d in cross:
        kb = lax.rem(x - k + NX, NX) * 2 + (c if d == 0 else other)
        arrived(posk.at[kb], ksem_r.at[2 * k + d])
    for kb in range(8):
        poskt[kb] = jnp.broadcast_to(posk[kb].astype(F32), (TOK, TOK)).T
    for k in range(1, NZ):
        arrived(og_all.at[rows(lax.rem(z - k + NZ, NZ), TOK)], osem_r.at[k])
    for k in range(1, NZ):
        arrived(q_all.at[rows(lax.rem(z - k + NZ, NZ), TOK)], qsem_r.at[k])
    place_q = jnp.concatenate([posq[i].astype(F32) for i in range(NZ)], 1)

    def block_of(k):
        return lax.rem(x - k // 2 + NX, NX) * 2 + lax.rem(c + lax.rem(k, 2), 2)

    def first(k, carry):
        kb = block_of(k)

        @pl.when(k > 0)
        def _():
            arrived(kv_all.at[kb], kvsem_r.at[k])

        key = kv_all[kb, :, :HEAD_DIM]
        value = kv_all[kb, :, HEAD_DIM:]
        kt_all[kb] = key.T
        pk = poskt[kb]
        pk = jnp.concatenate([pk, pk], 1)
        for j in range(4):
            cols = pl.ds(j * 256, 256)
            s = nt(key, q_all[cols, :])
            dp = nt(value, og_all[cols, :])
            s = jnp.where(place_q[:, j * 256 : (j + 1) * 256] >= pk, s, LOW)
            top = jnp.max(s, 0, keepdims=True)
            e = jnp.exp2((s - top) * EXP2_SCALE)
            e_all[kb, :, cols] = e
            dp_all[kb, :, cols] = dp
            mb[pl.ds(kb, 1), cols] = top
            lb[pl.ds(kb, 1), cols] = jnp.sum(e, 0, keepdims=True)
            ab[pl.ds(kb, 1), cols] = jnp.sum(e * dp, 0, keepdims=True)
        return carry

    lax.fori_loop(0, 8, first, 0)
    top = jnp.max(mb[...], 0, keepdims=True)
    fade = jnp.exp2((mb[...] - top) * EXP2_SCALE)
    st_all[z, 0:1, :] = top
    st_all[z, 1:2, :] = jnp.sum(lb[...] * fade, 0, keepdims=True)
    st_all[z, 2:3, :] = jnp.sum(ab[...] * fade, 0, keepdims=True)
    st_all[z, 3:4, :] = jnp.zeros((1, 1024), F32)
    for k in range(1, NZ):
        blk = st_all.at[z]
        send(blk, blk, ssem_s.at[k], ssem_r.at[k], zpeer(k))

    lx.wait()
    for k, d in cross:
        b = lax.rem(y - k + NY, NY) * 2 + (c if d == 0 else other)
        arrived(actx.at[b], asem_r.at[2 * k + d])

    def turn_block(b, carry):
        actxt[:, pl.ds(pl.multiple_of(b * TOK, TOK), TOK)] = actx[b].T
        return carry

    lax.fori_loop(0, 8, turn_block, 0)

    for k in range(1, NZ):
        arrived(st_all.at[lax.rem(z - k + NZ, NZ)], ssem_r.at[k])
    top = st_all[0, 0:1, :]
    for i in range(1, NZ):
        top = jnp.maximum(top, st_all[i, 0:1, :])
    total = jnp.zeros((1, 1024), F32)
    inner = jnp.zeros((1, 1024), F32)
    for i in range(NZ):
        fade = jnp.exp2((st_all[i, 0:1, :] - top) * EXP2_SCALE)
        total += st_all[i, 1:2, :] * fade
        inner += st_all[i, 2:3, :] * fade
    delta = inner / total
    mb[...] = jnp.exp2((mb[...] - top) * EXP2_SCALE) / total

    def second(k, carry):
        kb = block_of(k)
        dv = jnp.zeros((TOK, HEAD_DIM), F32)
        dk = jnp.zeros((TOK, HEAD_DIM), F32)
        for j in range(4):
            cols = pl.ds(j * 256, 256)
            p = e_all[kb, :, cols] * mb[pl.ds(kb, 1), cols]
            ds = (p * (dp_all[kb, :, cols] - delta[:, j * 256 : (j + 1) * 256])).astype(BF)
            ds_all[rows(kb, TOK), cols] = ds
            dv += nn(p.astype(BF), og_all[cols, :])
            dk += nn(ds, q_all[cols, :])
        dkv_out[kb, :, :HEAD_DIM] = (dk * SCALE).astype(BF)
        dkv_out[kb, :, HEAD_DIM:] = dv.astype(BF)

        @pl.when(k > 0)
        def _():
            pltpu.make_async_remote_copy(
                dkv_out.at[kb], dkv_in.at[xc], dkvsem_s.at[k], dkvsem_r.at[k],
                device_id=device(kb // 2, y, z, lax.rem(kb, 2)), device_id_type=MESH,
            ).start()

        return carry

    lax.fori_loop(0, 8, second, 0)
    kt = jnp.concatenate([kt_all[i] for i in range(8)], 1)
    for j in range(4):
        dq = nn(kt, ds_all[:, j * 256 : (j + 1) * 256]) * SCALE
        dq_out[2 * j] = dq[:, :TOK].astype(BF)
        dq_out[2 * j + 1] = dq[:, TOK:].astype(BF)
    for k in range(1, NZ):
        to = lax.rem(z + k, NZ)
        send(dq_out.at[to], dq_in.at[z], dqsem_s.at[k], dqsem_r.at[k], zpeer(k))

    dkv = dkv_out[xc].astype(F32)
    for k in range(1, 8):
        kb = lax.rem(x + k // 2, NX) * 2 + lax.rem(c + lax.rem(k, 2), 2)
        arrived(dkv_in.at[kb], dkvsem_r.at[k])
        dkv += dkv_in[kb].astype(F32)
    dkey = dkv[:, :HEAD_DIM]
    dkey = dkey * cosine - turn(dkey) * sine
    dq = dq_out[z].astype(F32)
    for k in range(1, NZ):
        frm = lax.rem(z - k + NZ, NZ)
        arrived(dq_in.at[frm], dqsem_r.at[k])
        dq += dq_in[frm].astype(F32)
    dq = dq.T
    dq = dq * cosine - turn(dq) * sine
    gp_all[yc, :, :HEAD_DIM] = dq.astype(BF)
    gp_all[yc, :, HEAD_DIM : 2 * HEAD_DIM] = dkey.astype(BF)
    gp_all[yc, :, 2 * HEAD_DIM :] = dkv[:, HEAD_DIM:].astype(BF)

    blk = gp_all.at[yc]
    for k in (2, 1, 3):
        send(blk, blk, gsem_s.at[0, k], gsem_r.at[0, k], ypeer(k))
    send(blk, blk, gsem_s.at[1, 0], gsem_r.at[1, 0], sibling)

    def acts_grad(j, carry):
        cols = pl.ds(pl.multiple_of(j * 512, 512), 512)
        ga_v[:, cols] = nt(gp_all[yc], w_v[cols, :])
        return carry

    lax.fori_loop(0, 8, acts_grad, 0)
    lga = pltpu.make_async_copy(ga_v, ga_hbm.at[0], lsem.at[6])
    lga.start()
    for k in (1, 3, 2):
        blk = gp_all.at[lax.rem(y - k + NY, NY) * 2 + c]
        arrived(blk, gsem_r.at[0, k])
        send(blk, blk, gsem_s.at[1, k], gsem_r.at[1, k], sibling)
    for k in range(4):
        blk = gp_all.at[lax.rem(y - k + NY, NY) * 2 + other]
        arrived(blk, gsem_r.at[1, k])
    gp = gp_all[...].reshape(8 * TOK, WIDE)
    for i in range(NX):
        dw = nn(actxt[i * 128 : (i + 1) * 128, :], gp)
        dwx_out[i] = dw.astype(BF)

    for k in (2, 1, 3):
        to = lax.rem(x + k, NX)
        send(dwx_out.at[to], dwx_in.at[x], xsem_s.at[k], xsem_r.at[k], xpeer(k))
    dw = dwx_out[x].astype(F32)
    for k in (1, 3, 2):
        frm = lax.rem(x - k + NX, NX)
        arrived(dwx_in.at[frm], xsem_r.at[k])
        dw += dwx_in[frm].astype(F32)
    dwz_out[...] = dw.astype(BF).reshape(8, 16, WIDE)
    for k in (4, 3, 5, 2, 6, 1, 7):
        to = lax.rem(z + k, NZ)
        send(dwz_out.at[to], dwz_in.at[z], zsem_s.at[k], zsem_r.at[k], zpeer(k))
    dw = dwz_out[z].astype(F32)
    for k in range(1, NZ):
        frm = lax.rem(z - k + NZ, NZ)
        arrived(dwz_in.at[frm], zsem_r.at[k])
        dw += dwz_in[frm].astype(F32)

    def piece(zz):
        return pl.ds(pl.multiple_of(c * 512 + x * 128 + zz * 16, 16), 16)

    def band(xx, cc):
        return dw_all.at[pl.ds(pl.multiple_of(cc * 512 + xx * 128, 128), 128)]

    dw_all[piece(z), :] = dw.astype(BF)
    for k in (4, 3, 5, 2, 6, 1, 7):
        blk = dw_all.at[piece(z)]
        send(blk, blk, zgsem_s.at[k], zgsem_r.at[k], zpeer(k))
    for k in range(1, NZ):
        arrived(dw_all.at[piece(lax.rem(z - k + NZ, NZ))], zgsem_r.at[k])
    blk = band(x, c)
    for k in (2, 1, 3):
        send(blk, blk, xgsem_s.at[0, k], xgsem_r.at[0, k], xpeer(k))
    send(blk, blk, xgsem_s.at[1, 0], xgsem_r.at[1, 0], sibling)
    for k in (1, 3, 2):
        blk = band(lax.rem(x - k + NX, NX), c)
        arrived(blk, xgsem_r.at[0, k])
        send(blk, blk, xgsem_s.at[1, k], xgsem_r.at[1, k], sibling)
    for k in (0, 1, 3, 2):
        arrived(band(lax.rem(x - k + NX, NX), other), xgsem_r.at[1, k])
    gw_v[...] = dw_all[...].astype(F32)
    lgw = pltpu.make_async_copy(gw_v, gw_hbm, lsem.at[7])
    lgw.start()

    for k in range(1, 8):
        pltpu.make_async_remote_copy(
            dkv_out.at[0], dkv_in.at[0], dkvsem_s.at[k], dkvsem_r.at[k],
            device_id=sibling, device_id_type=MESH,
        ).wait_send()
    for cp in sends:
        cp.wait_send()
    lga.wait()
    lgw.wait()


def shards(activations, weights, positions, out_grad):
    steps = np.arange(HEAD_DIM // 2, dtype=np.float64)
    freq = (ROPE_BASE ** (-(steps * 2.0 / HEAD_DIM))).astype(np.float32)
    freq = jnp.asarray(np.concatenate([freq, freq])[None])
    hbm = pl.BlockSpec(memory_space=pl.ANY)
    dma = pltpu.SemaphoreType.DMA
    V = pltpu.VMEM
    scratch = [
        V((TOK, 4096), BF), V((4096, WIDE), BF), V((1024, HEAD_DIM), BF), V((1024, HEAD_DIM), BF),
        V((NZ, 1, TOK), jnp.int32), V((8, 1, TOK), jnp.int32), V((8, TOK, TOK), F32),
        V((8, TOK, 2 * HEAD_DIM), BF), V((8, HEAD_DIM, TOK), BF), V((TOK, WIDE), F32),
        V((8, TOK, 1024), F32), V((8, TOK, 1024), F32), V((1024, 1024), BF),
        V((8, 1024), F32), V((8, 1024), F32), V((8, 1024), F32), V((NZ, 4, 1024), F32),
        V((NZ, HEAD_DIM, TOK), BF), V((NZ, HEAD_DIM, TOK), BF),
        V((8, TOK, 2 * HEAD_DIM), BF), V((8, TOK, 2 * HEAD_DIM), BF),
        V((8, TOK, WIDE), BF), V((8, TOK, 512), BF), V((512, 1024), BF),
        V((NX, 128, WIDE), BF), V((NX, 128, WIDE), BF), V((8, 128), F32),
        V((NZ, 16, WIDE), BF), V((NZ, 16, WIDE), BF), V((1024, WIDE), BF),
        V((TOK, 4096), F32), V((1024, WIDE), F32),
        dma((8,)), dma((2, 2, 4)), dma((2, 2, 4)), dma((8,)), dma((8,)), dma((8,)), dma((8,)),
        dma((8,)), dma((8,)), dma((8,)), dma((8,)), dma((8,)), dma((8,)), dma((8,)), dma((8,)),
        dma((8,)), dma((8,)), dma((8,)), dma((8,)), dma((8,)), dma((8,)), dma((2, 4)), dma((2, 4)),
        dma((4,)), dma((4,)), dma((8,)), dma((8,)), dma((8,)), dma((8,)), dma((2, 4)), dma((2, 4)),
    ]
    return tuple(
        pl.pallas_call(
            kernel,
            out_shape=(
                jax.ShapeDtypeStruct((1, TOK, 4096), F32),
                jax.ShapeDtypeStruct((1024, WIDE), F32),
            ),
            in_specs=[pl.BlockSpec(memory_space=pltpu.VMEM)] + [hbm] * 4,
            out_specs=(hbm, hbm),
            scratch_shapes=scratch,
            compiler_params=pltpu.CompilerParams(
                collective_id=0, has_side_effects=True, vmem_limit_bytes=56 << 20
            ),
        )(freq, activations, weights, positions, out_grad)
    )


def solution(mesh):
    placed = (
        P("dp", ("outer", "inner"), None),
        P("dp", None),
        P("dp", ("outer", "inner")),
        P("dp", ("outer", "inner"), None),
    )
    return jax.shard_map(
        shards,
        mesh=mesh,
        in_specs=placed,
        out_specs=(P("dp", ("outer", "inner"), None), P("dp", None)),
        check_vma=False,
    )
```

```python
import jax
import jax.numpy as jnp
import numpy as np
from jax import lax
from jax.experimental import pallas as pl
from jax.experimental.pallas import tpu as pltpu
from jax.sharding import PartitionSpec as P

HEAD_DIM = 128
ROPE_BASE = 500000.0
NX, NY, NZ, NC = 4, 4, 8, 2
TOK = 128
WIDE = 3 * HEAD_DIM
MESH = pl.DeviceIdType.MESH
BF = jnp.bfloat16
F32 = jnp.float32
SCALE = HEAD_DIM ** (-0.5)
EXP2_SCALE = SCALE * 1.4426950408889634
LOW = -1e30
STEPS = ((0, 0), (0, 1), (1, 0), (3, 0), (2, 0), (1, 1), (3, 1), (2, 1))


def coords():
    outer, inner = lax.axis_index("outer"), lax.axis_index("inner")
    return (
        (outer // 2) * 2 + lax.rem(inner, 2),
        lax.axis_index("dp"),
        inner // 2,
        lax.rem(outer, 2),
    )


def device(x, y, z, c):
    return {"dp": y, "outer": (x // 2) * 2 + c, "inner": z * 2 + lax.rem(x, 2)}


def nt(a, b):
    return lax.dot_general(a, b, (((1,), (1,)), ((), ())), preferred_element_type=F32)


def nn(a, b):
    return lax.dot_general(a, b, (((1,), (0,)), ((), ())), preferred_element_type=F32)


def turn(u):
    lane = lax.broadcasted_iota(jnp.int32, u.shape, 1)
    half = jnp.roll(u, HEAD_DIM // 2, 1) if False else pltpu.roll(u, HEAD_DIM // 2, 1)
    return jnp.where(lane < HEAD_DIM // 2, -half, half)


def kernel(
    freq_hbm, act_hbm, w_hbm, pos_hbm, og_hbm, ga_ref, gw_ref,
    freq_v, act_v, w_v, og_all, q_all, posq, posk, poskt, kv_all, kt_all, proj,
    e_all, dp_all, ds_all, mb, lb, ab, dl, acc, p_all, st_all,
    dq_out, dq_in, dkv_out, dkv_in, gp_all, actx, actxt,
    dwx_out, dwx_in, mark, dwz_out, dwz_in, dw_all,
    sent, lsem, wsem_y, wsem_x, wsem_c, psem, ksem, osem, qsem, kvsem_x, kvsem_c, asem, ssem,
    dqsem, dkvsem, gsem_y, gsem_c, xsem, zsem, zgsem, xgsem, sgsem,
):
    x, y, z, c = coords()
    other = 1 - c
    xc, yc = x * 2 + c, y * 2 + c
    sends = []

    def xpeer(k):
        return device(lax.rem(x + k, NX), y, z, c)

    def ypeer(k):
        return device(x, lax.rem(y + k, NY), z, c)

    def zpeer(k):
        return device(x, y, lax.rem(z + k, NZ), c)

    sibling = device(x, y, z, other)

    def send(src, dst, rs, dev):
        cp = pltpu.make_async_remote_copy(src, dst, sent, rs, device_id=dev, device_id_type=MESH)
        cp.start()
        sends.append(cp)

    def arrived(dst, rs):
        pltpu.make_async_remote_copy(
            dst, dst, rs, rs, device_id=sibling, device_id_type=MESH
        ).wait_recv()

    def rows(i, n):
        return pl.ds(pl.multiple_of(i * n, n), n)

    cross = [(k, d) for k in range(4) for d in range(2)][1:]

    lw = pltpu.make_async_copy(w_hbm, w_v.at[rows(y, 1024)], lsem.at[0])
    lw.start()
    lp = pltpu.make_async_copy(pos_hbm, posq.at[z], lsem.at[1])
    lp.start()
    lo = pltpu.make_async_copy(og_hbm.at[0], og_all.at[rows(z, TOK)], lsem.at[1])
    lo.start()
    la = pltpu.make_async_copy(act_hbm.at[0], act_v, lsem.at[2])
    la.start()
    lk = pltpu.make_async_copy(pos_hbm, posk.at[xc], lsem.at[1])
    lk.start()
    lf = pltpu.make_async_copy(freq_hbm, freq_v, lsem.at[1])
    lf.start()

    barrier = pltpu.get_barrier_semaphore()
    greet = [sibling] + [zpeer(k) for k in range(1, NZ)]
    for k in range(1, 4):
        greet += [xpeer(k), ypeer(k)]
        greet += [
            device(lax.rem(x + k, NX), y, z, other),
            device(x, lax.rem(y + k, NY), z, other),
        ]
    for dev in greet:
        pl.semaphore_signal(barrier, inc=1, device_id=dev, device_id_type=MESH)
    pl.semaphore_wait(barrier, len(greet))

    KVC, QC = pl.ds(HEAD_DIM, 2 * HEAD_DIM), pl.ds(0, HEAD_DIM)
    COLS = (QC, KVC)
    YORDER = (1, 3, 2)
    odd = lax.rem(x, 2)
    near, far = odd * 2 + c, (1 - odd) * 2 + c
    near_sib, far_sib = odd * 2 + other, (1 - odd) * 2 + other

    def wblock(owner, piece, cols, start=0, n=256):
        first_row = pl.multiple_of(owner * 1024 + piece * 256 + start, n)
        return w_v.at[pl.ds(first_row, n), cols]

    def wshare(part, k):
        owner, cols = lax.rem(y - k + NY, NY), COLS[part]
        blk = wblock(owner, near, cols)
        arrived(blk, wsem_y.at[part, k])
        if part == 1 and k != 2:
            half = wblock(owner, near, cols, 0 if k == 1 else 128, 128)
            send(half, half, wsem_y.at[part, 2], ypeer(k))
        for i, d in enumerate((1, 3)):
            half = wblock(owner, near, cols, i * 128, 128)
            send(half, half, wsem_x.at[part, k], xpeer(d))
        send(blk, blk, wsem_c.at[part, k], sibling)

    def wpass(part, k):
        owner, cols = lax.rem(y - k + NY, NY), COLS[part]
        blk = wblock(owner, far, cols)
        arrived(blk, wsem_x.at[part, k])
        send(blk, blk, wsem_c.at[part, k], sibling)

    def wuse(part, k):
        owner, cols = lax.rem(y - k + NY, NY), COLS[part]
        arrived(w_v.at[pl.ds(0, 512), cols], wsem_c.at[part, k])
        proj[:, cols] += nn(acts(owner), w_v[rows(owner, 1024), cols])

    lw.wait()
    for part in range(2):
        for k in (1, 3) if part else YORDER:
            blk = wblock(y, near, COLS[part])
            send(blk, blk, wsem_y.at[part, k], ypeer(k))
    lo.wait()
    lp.wait()
    lk.wait()
    lf.wait()
    for k in range(1, NZ):
        blk = posq.at[z]
        send(blk, blk, psem, zpeer(k))
    for k, d in cross:
        blk = posk.at[xc]
        dev = device(lax.rem(x + k, NX), y, z, c if d == 0 else other)
        send(blk, blk, ksem, dev)
    for k in range(1, NZ):
        blk = og_all.at[rows(z, TOK)]
        send(blk, blk, osem, zpeer(k))

    place = posq[z].astype(F32)
    angles = jnp.broadcast_to(place, (TOK, HEAD_DIM)).T * freq_v[...]
    cosine, sine = jnp.cos(angles), jnp.sin(angles)

    la.wait()

    def acts(owner):
        return act_v[:, pl.ds(pl.multiple_of(owner * 1024, 1024), 1024)]

    proj[...] = nn(acts(y), w_v[rows(y, 1024), :])
    for k in YORDER:
        wshare(0, k)
    wshare(1, 1)
    wshare(1, 3)
    for k in YORDER:
        wpass(0, k)
    for k in YORDER:
        wuse(0, k)
    queries = proj[:, :HEAD_DIM]
    queries = queries * cosine + turn(queries) * sine
    q_all[rows(z, TOK), :] = queries.astype(BF)
    for k in range(1, NZ):
        blk = q_all.at[rows(z, TOK)]
        send(blk, blk, qsem, zpeer(k))
    wshare(1, 2)
    wpass(1, 1)
    wpass(1, 3)
    wuse(1, 1)
    wuse(1, 3)
    wpass(1, 2)
    wuse(1, 2)
    keys = proj[:, HEAD_DIM : 2 * HEAD_DIM]
    keys = keys * cosine + turn(keys) * sine
    kv_all[xc, :, :HEAD_DIM] = keys.astype(BF)
    kv_all[xc, :, HEAD_DIM:] = proj[:, 2 * HEAD_DIM :].astype(BF)
    blk = kv_all.at[xc]
    for k in (2, 1, 3):
        send(blk, blk, kvsem_x.at[k], xpeer(k))
    send(blk, blk, kvsem_c.at[0], sibling)

    for k, d in cross:
        to_y, to_c = lax.rem(y + k, NY), c if d == 0 else other
        src = act_v.at[:, pl.ds(pl.multiple_of(to_y * 1024 + to_c * 512, 512), 512)]
        send(src, actx.at[yc], asem, device(x, to_y, z, to_c))
    lx = pltpu.make_async_copy(
        act_v.at[:, pl.ds(pl.multiple_of(y * 1024 + c * 512, 512), 512)], actx.at[yc], lsem.at[3]
    )
    lx.start()

    arrived(posq.at[pl.ds(0, 7)], psem)
    arrived(posk.at[pl.ds(0, 7)], ksem)
    for kb in range(8):
        poskt[kb] = jnp.broadcast_to(posk[kb].astype(F32), (TOK, TOK)).T
    arrived(og_all.at[pl.ds(0, 7 * TOK)], osem)
    arrived(q_all.at[pl.ds(0, 7 * TOK)], qsem)
    place_q = jnp.concatenate([posq[i].astype(F32) for i in range(NZ)], 1)

    def step_of(j):
        i = lax.rem(j + 1, 3)
        dx = jnp.where(j < 2, 0, lax.rem(1 + 2 * i, 4) + i // 2)
        return dx, jnp.where(j < 2, j, (j - 2) // 3)

    def block_of(j):
        dx, dc = step_of(j)
        return lax.rem(x - dx + NX, NX) * 2 + lax.rem(c + dc, 2)

    def relay(k):
        blk = kv_all.at[lax.rem(x - k + NX, NX) * 2 + c]
        arrived(blk, kvsem_x.at[k])
        send(blk, blk, kvsem_c.at[k], sibling)

    def first(k, carry, half):
        kb = block_of(k)
        dx, dc = step_of(k)
        key = kv_all.at[kb, :, pl.ds(0, HEAD_DIM)]
        value = kv_all.at[kb, :, pl.ds(HEAD_DIM, HEAD_DIM)]
        if half == 0:

            @pl.when(dc > 0)
            def _():
                arrived(kv_all.at[kb], kvsem_c.at[dx])

            kt_all[kb] = key[...].T
        pk = poskt[kb]
        pk = jnp.concatenate([pk, pk], 1)
        for j in (2 * half, 2 * half + 1):
            cols = pl.ds(j * 256, 256)
            s = nt(key[...], q_all[cols, :])
            dp = nt(value[...], og_all[cols, :])
            s = jnp.where(place_q[:, j * 256 : (j + 1) * 256] >= pk, s, LOW)
            top = jnp.max(s, 0, keepdims=True)
            e = jnp.exp2((s - top) * EXP2_SCALE)
            e_all[kb, :, cols] = e
            dp_all[kb, :, cols] = dp
            mb[pl.ds(kb, 1), cols] = top
            lb[pl.ds(kb, 1), cols] = jnp.sum(e, 0, keepdims=True)
            ab[pl.ds(kb, 1), cols] = jnp.sum(e * dp, 0, keepdims=True)
        return carry

    def first_half(k, carry):
        return first(k, carry, 0)

    def other_half(k, carry):
        return first(k, carry, 1)

    def stats_send(half):
        cols = pl.ds(half * 512, 512)
        high = mb[:, cols]
        top = jnp.max(high, 0, keepdims=True)
        fade = jnp.exp2((high - top) * EXP2_SCALE)
        total = jnp.sum(lb[:, cols] * fade, 0, keepdims=True)
        st_all[half, z, 0:1, :] = top * EXP2_SCALE + jnp.log2(total)
        st_all[half, z, 1:2, :] = jnp.sum(ab[:, cols] * fade, 0, keepdims=True) / total
        blk = st_all.at[half, z]
        for k in range(1, NZ):
            send(blk, blk, ssem.at[half], zpeer(k))

    def stats_merge(half):
        cols = pl.ds(half * 512, 512)
        arrived(st_all.at[half, pl.ds(0, 7)], ssem.at[half])
        top = st_all[half, 0, 0:1, :]
        for i in range(1, NZ):
            top = jnp.maximum(top, st_all[half, i, 0:1, :])
        total = jnp.zeros((1, 512), F32)
        delta = jnp.zeros((1, 512), F32)
        for i in range(NZ):
            fade = jnp.exp2(st_all[half, i, 0:1, :] - top)
            total += fade
            delta += st_all[half, i, 1:2, :] * fade
        dl[:, cols] = delta / total
        mb[:, cols] = jnp.exp2(mb[:, cols] * EXP2_SCALE - (top + jnp.log2(total)))

    def grads_of(kb, j):
        cols = pl.ds(j * 256, 256)
        p = e_all[kb, :, cols] * mb[pl.ds(kb, 1), cols]
        ds = (p * (dp_all[kb, :, cols] - dl[:, cols])).astype(BF)
        ds_all[rows(kb, TOK), cols] = ds
        return p.astype(BF), ds

    def dq_send(half):
        kt = jnp.concatenate([kt_all[i] for i in range(8)], 1)
        for j in (2 * half, 2 * half + 1):
            dq = nn(kt, ds_all[:, j * 256 : (j + 1) * 256]) * SCALE
            dq_out[2 * j] = dq[:, :TOK].astype(BF)
            dq_out[2 * j + 1] = dq[:, TOK:].astype(BF)
        for to in range(4 * half, 4 * half + 4):

            @pl.when(z != to)
            def _():
                pltpu.make_async_remote_copy(
                    dq_out.at[to], dq_in.at[z], sent, dqsem,
                    device_id=device(x, y, to, c), device_id_type=MESH,
                ).start()

    lax.fori_loop(0, 2, first_half, 0, unroll=True)
    relay(1)
    relay(3)
    lax.fori_loop(2, 4, first_half, 0, unroll=True)
    relay(2)
    lax.fori_loop(4, 8, first_half, 0, unroll=True)
    stats_send(0)
    lax.fori_loop(0, 8, other_half, 0, unroll=True)
    stats_send(1)
    stats_merge(0)

    def second_half0(k, carry):
        dv = jnp.zeros((TOK, HEAD_DIM), F32)
        dk = jnp.zeros((TOK, HEAD_DIM), F32)
        for j in range(2):
            cols = pl.ds(j * 256, 256)
            p, ds = grads_of(k, j)
            dv += nn(p, og_all[cols, :])
            dk += nn(ds, q_all[cols, :])
        acc[k, :, :HEAD_DIM] = dk
        acc[k, :, HEAD_DIM:] = dv
        return carry

    lax.fori_loop(0, 8, second_half0, 0, unroll=True)
    dq_send(0)
    stats_merge(1)

    def second_half1(k, carry):
        for j in range(2, 4):
            p, ds = grads_of(k, j)
            p_all[k, :, pl.ds((j - 2) * 256, 256)] = p
        return carry

    lax.fori_loop(0, 8, second_half1, 0, unroll=True)
    dq_send(1)

    def key_grads(i, carry):
        k = 7 - i
        kb = block_of(k)
        dk = acc[kb, :, :HEAD_DIM] + nn(ds_all[rows(kb, TOK), 512:], q_all[512:, :])
        dv = acc[kb, :, HEAD_DIM:] + nn(p_all[kb], og_all[512:, :])
        dkv_out[kb, :, :HEAD_DIM] = (dk * SCALE).astype(BF)
        dkv_out[kb, :, HEAD_DIM:] = dv.astype(BF)

        @pl.when(k > 0)
        def _():
            pltpu.make_async_remote_copy(
                dkv_out.at[kb], dkv_in.at[xc], sent, dkvsem,
                device_id=device(kb // 2, y, z, lax.rem(kb, 2)), device_id_type=MESH,
            ).start()

        return carry

    lax.fori_loop(0, 8, key_grads, 0, unroll=True)
    lx.wait()
    arrived(actx.at[pl.ds(0, 7)], asem)

    def turn_block(b, carry):
        actxt[:, pl.ds(pl.multiple_of(b * TOK, TOK), TOK)] = actx[b].T
        return carry

    lax.fori_loop(0, 8, turn_block, 0)
    arrived(dkv_in.at[pl.ds(0, 7)], dkvsem)
    dkv = dkv_out[xc].astype(F32)
    for k in range(1, 8):
        dkv += dkv_in[lax.rem(xc + k, 8)].astype(F32)
    dkey = dkv[:, :HEAD_DIM]
    dkey = dkey * cosine - turn(dkey) * sine
    gp_all[yc, :, HEAD_DIM : 2 * HEAD_DIM] = dkey.astype(BF)
    gp_all[yc, :, 2 * HEAD_DIM :] = dkv[:, HEAD_DIM:].astype(BF)

    def third(i):
        return pl.ds(i * HEAD_DIM, HEAD_DIM)

    def gp_send(i):
        blk = gp_all.at[yc, :, third(i)]
        for k in (2, 1, 3):
            send(blk, blk, gsem_y.at[i, k], ypeer(k))
        send(blk, blk, gsem_c.at[i], sibling)

    def gp_relay(i):
        for k in YORDER:
            blk = gp_all.at[lax.rem(y - k + NY, NY) * 2 + c, :, third(i)]
            arrived(blk, gsem_y.at[i, k])
            send(blk, blk, gsem_c.at[i], sibling)

    def dw_send(i):
        arrived(gp_all.at[pl.ds(0, 4), :, third(i)], gsem_c.at[i])
        gp = gp_all[:, :, third(i)].reshape(8 * TOK, HEAD_DIM)
        for j in range(NX):
            dwx_out[i, j] = nn(actxt[j * 128 : (j + 1) * 128, :], gp).astype(BF)
        for k in (2, 1, 3):
            to = lax.rem(x + k, NX)
            send(dwx_out.at[i, to], dwx_in.at[i, x], xsem.at[i], xpeer(k))

    def band_send(i):
        arrived(dwx_in.at[i, pl.ds(0, 3)], xsem.at[i])
        dw = dwx_out[i, x].astype(F32)
        for k in range(1, NX):
            dw += dwx_in[i, lax.rem(x + k, NX)].astype(F32)
        dwz_out[i] = dw.astype(BF).reshape(8, 16, HEAD_DIM)
        for k in (4, 3, 5, 2, 6, 1, 7):
            to = lax.rem(z + k, NZ)
            send(dwz_out.at[i, to], dwz_in.at[i, z], zsem.at[i], zpeer(k))

    def band(i, xx, cc):
        return dw_all.at[i, pl.ds(pl.multiple_of(cc * 512 + xx * 128, 128), 128)]

    def piece_send(i):
        arrived(dwz_in.at[i, pl.ds(0, 7)], zsem.at[i])
        dw = dwz_out[i, z].astype(F32)
        for k in range(1, NZ):
            dw += dwz_in[i, lax.rem(z + k, NZ)].astype(F32)
        own = pl.ds(pl.multiple_of(c * 512 + x * 128 + z * 16, 16), 16)
        dw_all[i, own, :] = dw.astype(BF)
        blk = dw_all.at[i, own]
        for k in (4, 3, 5, 2, 6, 1, 7):
            send(blk, blk, zgsem.at[i], zpeer(k))

    def spread(i):
        arrived(dw_all.at[i, pl.ds(0, 7 * 16)], zgsem.at[i])
        blk = band(i, x, c)
        for k in (2, 1, 3):
            send(blk, blk, xgsem.at[i, k], xpeer(k))
        send(blk, blk, sgsem.at[i], sibling)

    def spread_relay(i):
        for k in (1, 3, 2):
            blk = band(i, lax.rem(x - k + NX, NX), c)
            arrived(blk, xgsem.at[i, k])
            send(blk, blk, sgsem.at[i], sibling)

    def finish(i):
        arrived(dw_all.at[i, pl.ds(0, 512)], sgsem.at[i])
        gw_ref[:, third(i)] = dw_all[i].astype(F32)

    gp_send(2)
    gp_send(1)
    arrived(dq_in.at[pl.ds(0, 7)], dqsem)
    dq = dq_out[z].astype(F32)
    for k in range(1, NZ):
        dq += dq_in[lax.rem(z + k, NZ)].astype(F32)
    dq = dq.T
    dq = dq * cosine - turn(dq) * sine
    gp_all[yc, :, :HEAD_DIM] = dq.astype(BF)
    gp_send(0)

    def acts_grad(j, carry):
        cols = pl.ds(pl.multiple_of(j * 512, 512), 512)
        ga_ref[0, :, cols] = nt(gp_all[yc], w_v[cols, :])
        return carry

    lax.fori_loop(0, 8, acts_grad, 0)
    gp_relay(2)
    dw_send(2)
    gp_relay(1)
    dw_send(1)
    gp_relay(0)
    dw_send(0)
    band_send(2)
    band_send(1)
    band_send(0)
    piece_send(2)
    piece_send(1)
    piece_send(0)
    spread(2)
    spread(1)
    spread(0)
    spread_relay(2)
    spread_relay(1)
    finish(2)
    spread_relay(0)
    finish(1)
    finish(0)

    for out, sem in ((dkv_out, dkvsem), (dq_out, dqsem)):
        blk = out.at[pl.ds(0, 7)]
        pltpu.make_async_remote_copy(
            blk, blk, sent, sem, device_id=sibling, device_id_type=MESH
        ).wait_send()
    for cp in sends:
        cp.wait_send()


def put(ga_ref, gw_ref, ga_hbm, gw_hbm, sem):
    copies = []
    for i in range(2):
        part = pl.ds(i * 64, 64)
        copies.append(pltpu.make_async_copy(ga_ref.at[0, part], ga_hbm.at[0, part], sem.at[0, i]))
        part = pl.ds(i * 512, 512)
        copies.append(pltpu.make_async_copy(gw_ref.at[part], gw_hbm.at[part], sem.at[1, i]))
    for cp in copies:
        cp.start()
    for cp in copies:
        cp.wait()


def shards(activations, weights, positions, out_grad):
    steps = np.arange(HEAD_DIM // 2, dtype=np.float64)
    freq = (ROPE_BASE ** (-(steps * 2.0 / HEAD_DIM))).astype(np.float32)
    freq = jnp.asarray(np.concatenate([freq, freq])[None])
    operands = (freq, activations, weights, positions, out_grad)
    hbm = pl.BlockSpec(memory_space=pltpu.HBM)
    vmem = pl.BlockSpec(memory_space=pltpu.VMEM)
    dma = pltpu.SemaphoreType.DMA
    V = pltpu.VMEM
    scratch = [
        V((1, HEAD_DIM), F32), V((TOK, 4096), BF), V((4096, WIDE), BF), V((1024, HEAD_DIM), BF), V((1024, HEAD_DIM), BF),
        V((NZ, 1, TOK), jnp.int32), V((8, 1, TOK), jnp.int32), V((8, TOK, TOK), F32),
        V((8, TOK, 2 * HEAD_DIM), BF), V((8, HEAD_DIM, TOK), BF), V((TOK, WIDE), F32),
        V((8, TOK, 1024), F32), V((8, TOK, 1024), F32), V((1024, 1024), BF),
        V((8, 1024), F32), V((8, 1024), F32), V((8, 1024), F32), V((1, 1024), F32),
        V((8, TOK, 2 * HEAD_DIM), F32), V((8, TOK, 512), BF), V((2, NZ, 2, 512), F32),
        V((NZ, HEAD_DIM, TOK), BF), V((NZ, HEAD_DIM, TOK), BF),
        V((8, TOK, 2 * HEAD_DIM), BF), V((8, TOK, 2 * HEAD_DIM), BF),
        V((8, TOK, WIDE), BF), V((8, TOK, 512), BF), V((512, 1024), BF),
        V((3, NX, 128, 128), BF), V((3, NX, 128, 128), BF), V((8, 128), F32),
        V((3, NZ, 16, 128), BF), V((3, NZ, 16, 128), BF), V((3, 1024, 128), BF),
        dma(()), dma((4,)), dma((2, 4)), dma((2, 4)), dma((2, 4)), dma(()), dma(()), dma(()), dma(()),
        dma((4,)), dma((4,)), dma(()), dma((2,)), dma(()), dma(()), dma((3, 4)), dma((3,)), dma((3,)),
        dma((3,)), dma((3,)), dma((3, 4)), dma((3,)),
    ]
    grads = pl.pallas_call(
        kernel,
        out_shape=(pltpu.VMEM((1, TOK, 4096), F32), pltpu.VMEM((1024, WIDE), F32)),
        in_specs=[hbm] * 5,
        out_specs=(vmem, vmem),
        scratch_shapes=scratch,
        compiler_params=pltpu.CompilerParams(
            collective_id=0, has_side_effects=True, vmem_limit_bytes=40 << 20
        ),
    )(*(pltpu.with_memory_space_constraint(a, pltpu.HBM) for a in operands))
    return pl.pallas_call(
        put,
        out_shape=(
            jax.ShapeDtypeStruct((1, TOK, 4096), F32),
            jax.ShapeDtypeStruct((1024, WIDE), F32),
        ),
        in_specs=[vmem, vmem],
        out_specs=(hbm, hbm),
        scratch_shapes=[dma((2, 2))],
        compiler_params=pltpu.CompilerParams(vmem_limit_bytes=8 << 20),
    )(*grads)


def solution(mesh):
    placed = (
        P("dp", ("outer", "inner"), None),
        P("dp", None),
        P("dp", ("outer", "inner")),
        P("dp", ("outer", "inner"), None),
    )
    return jax.shard_map(
        shards,
        mesh=mesh,
        in_specs=placed,
        out_specs=(P("dp", ("outer", "inner"), None), P("dp", None)),
        check_vma=False,
    )
```

```python
import jax
import jax.numpy as jnp
import numpy as np
from jax import lax
from jax.experimental import pallas as pl
from jax.experimental.pallas import tpu as pltpu
from jax.sharding import PartitionSpec as P

HEAD_DIM = 128
ROPE_BASE = 500000.0
NX, NY, NZ, NC = 4, 4, 8, 2
TOK = 128
WIDE = 3 * HEAD_DIM
MESH = pl.DeviceIdType.MESH
BF = jnp.bfloat16
F32 = jnp.float32
SCALE = HEAD_DIM ** (-0.5)
EXP2_SCALE = SCALE * 1.4426950408889634
LOW = -1e30
STEPS = ((0, 0), (0, 1), (1, 0), (3, 0), (2, 0), (1, 1), (3, 1), (2, 1))


def coords():
    outer, inner = lax.axis_index("outer"), lax.axis_index("inner")
    return (
        (outer // 2) * 2 + lax.rem(inner, 2),
        lax.axis_index("dp"),
        inner // 2,
        lax.rem(outer, 2),
    )


def device(x, y, z, c):
    return {"dp": y, "outer": (x // 2) * 2 + c, "inner": z * 2 + lax.rem(x, 2)}


def nt(a, b):
    return lax.dot_general(a, b, (((1,), (1,)), ((), ())), preferred_element_type=F32)


def nn(a, b):
    return lax.dot_general(a, b, (((1,), (0,)), ((), ())), preferred_element_type=F32)


def turn(u):
    lane = lax.broadcasted_iota(jnp.int32, u.shape, 1)
    half = jnp.roll(u, HEAD_DIM // 2, 1) if False else pltpu.roll(u, HEAD_DIM // 2, 1)
    return jnp.where(lane < HEAD_DIM // 2, -half, half)


def kernel(
    freq_hbm, act_hbm, w_hbm, pos_hbm, og_hbm, ga_ref, gw_ref,
    freq_v, act_v, w_v, og_all, q_all, posq, posk, poskt, k_all, v_all, kt_all, proj,
    e_all, dp_all, ds_all, mb, lb, ab, dl, acc_k, acc_v, p_all, st_all,
    dq_out, dq_in, acc_own, dc_out, dc_in, dx_out, dx_in, gp_all, actx, actxt,
    dwx_out, dwx_in, mark, dwz_out, dwz_in, dw_all,
    sent, lsem, wsem_y, wsem_x, wsem_c, psem, ksem, osem, qsem, kxsem, kcsem, vxsem, vcsem,
    asem, ssem,
    dqsem, dcsem, dxsem, gsem_y, gsem_c, xsem, zsem, zgsem, xgsem, sgsem,
):
    x, y, z, c = coords()
    other = 1 - c
    xc, yc = x * 2 + c, y * 2 + c
    sends = []

    def xpeer(k):
        return device(lax.rem(x + k, NX), y, z, c)

    def ypeer(k):
        return device(x, lax.rem(y + k, NY), z, c)

    def zpeer(k):
        return device(x, y, lax.rem(z + k, NZ), c)

    sibling = device(x, y, z, other)

    def send(src, dst, rs, dev):
        cp = pltpu.make_async_remote_copy(src, dst, sent, rs, device_id=dev, device_id_type=MESH)
        cp.start()
        sends.append(cp)

    def arrived(dst, rs):
        pltpu.make_async_remote_copy(
            dst, dst, rs, rs, device_id=sibling, device_id_type=MESH
        ).wait_recv()

    def rows(i, n):
        return pl.ds(pl.multiple_of(i * n, n), n)

    cross = [(k, d) for k in range(4) for d in range(2)][1:]

    lw = pltpu.make_async_copy(w_hbm, w_v.at[rows(y, 1024)], lsem.at[0])
    lw.start()
    lp = pltpu.make_async_copy(pos_hbm, posq.at[z], lsem.at[1])
    lp.start()
    lo = pltpu.make_async_copy(og_hbm.at[0], og_all.at[rows(z, TOK)], lsem.at[1])
    lo.start()
    la = pltpu.make_async_copy(act_hbm.at[0], act_v, lsem.at[2])
    la.start()
    lk = pltpu.make_async_copy(pos_hbm, posk.at[xc], lsem.at[1])
    lk.start()
    lf = pltpu.make_async_copy(freq_hbm, freq_v, lsem.at[1])
    lf.start()

    barrier = pltpu.get_barrier_semaphore()
    greet = [sibling] + [zpeer(k) for k in range(1, NZ)]
    for k in range(1, 4):
        greet += [xpeer(k), ypeer(k)]
        greet += [
            device(lax.rem(x + k, NX), y, z, other),
            device(x, lax.rem(y + k, NY), z, other),
        ]
    for dev in greet:
        pl.semaphore_signal(barrier, inc=1, device_id=dev, device_id_type=MESH)
    pl.semaphore_wait(barrier, len(greet))

    def third(i):
        return pl.ds(i * HEAD_DIM, HEAD_DIM)

    Q, K, V = range(3)
    YORDER = (1, 3, 2)
    odd = lax.rem(x, 2)
    near, far = odd * 2 + c, (1 - odd) * 2 + c
    near_sib, far_sib = odd * 2 + other, (1 - odd) * 2 + other

    def wblock(owner, piece, cols, start=0, n=256):
        first_row = pl.multiple_of(owner * 1024 + piece * 256 + start, n)
        return w_v.at[pl.ds(first_row, n), cols]

    def wshare(part, k):
        owner, cols = lax.rem(y - k + NY, NY), third(part)
        blk = wblock(owner, near, cols)
        arrived(blk, wsem_y.at[part, k - 1])
        if part != Q and k != 2:
            half = wblock(owner, near, cols, 0 if k == 1 else 128, 128)
            send(half, half, wsem_y.at[part, 1], ypeer(k))
        for i, d in enumerate((1, 3)):
            half = wblock(owner, near, cols, i * 128, 128)
            send(half, half, wsem_x.at[part, k - 1], xpeer(d))
        send(blk, blk, wsem_c.at[part, k - 1], sibling)

    def wpass(part, k):
        owner, cols = lax.rem(y - k + NY, NY), third(part)
        blk = wblock(owner, far, cols)
        arrived(blk, wsem_x.at[part, k - 1])
        send(blk, blk, wsem_c.at[part, k - 1], sibling)

    def wuse(part, k):
        owner, cols = lax.rem(y - k + NY, NY), third(part)
        arrived(w_v.at[pl.ds(0, 512), cols], wsem_c.at[part, k - 1])
        proj[:, cols] += nn(acts(owner), w_v[rows(owner, 1024), cols])

    lw.wait()
    for part in range(3):
        for k in (1, 3) if part else YORDER:
            blk = wblock(y, near, third(part))
            send(blk, blk, wsem_y.at[part, k - 1], ypeer(k))
    lo.wait()
    lp.wait()
    lk.wait()
    lf.wait()
    for k in range(1, NZ):
        blk = posq.at[z]
        send(blk, blk, psem, zpeer(k))
    for k, d in cross:
        blk = posk.at[xc]
        dev = device(lax.rem(x + k, NX), y, z, c if d == 0 else other)
        send(blk, blk, ksem, dev)
    for k in range(1, NZ):
        blk = og_all.at[rows(z, TOK)]
        send(blk, blk, osem, zpeer(k))

    place = posq[z].astype(F32)
    angles = jnp.broadcast_to(place, (TOK, HEAD_DIM)).T * freq_v[...]
    cosine, sine = jnp.cos(angles), jnp.sin(angles)

    la.wait()

    def acts(owner):
        return act_v[:, pl.ds(pl.multiple_of(owner * 1024, 1024), 1024)]

    proj[...] = nn(acts(y), w_v[rows(y, 1024), :])
    def along_x(blk, sem_x, sem_c):
        for k in (2, 1, 3):
            send(blk, blk, sem_x.at[k - 1], xpeer(k))
        send(blk, blk, sem_c.at[0], sibling)

    for k in YORDER:
        wshare(Q, k)
    wshare(K, 1)
    wshare(K, 3)
    wpass(Q, 1)
    wpass(Q, 3)
    wshare(V, 1)
    wshare(V, 3)
    wpass(Q, 2)
    wshare(K, 2)
    for k in YORDER:
        wuse(Q, k)
    queries = proj[:, third(Q)]
    queries = queries * cosine + turn(queries) * sine
    q_all[rows(z, TOK), :] = queries.astype(BF)
    for k in range(1, NZ):
        blk = q_all.at[rows(z, TOK)]
        send(blk, blk, qsem, zpeer(k))
    wshare(V, 2)
    for k in YORDER:
        wpass(K, k)
    wpass(V, 1)
    wpass(V, 3)
    for k in YORDER:
        wuse(K, k)
    keys = proj[:, third(K)]
    keys = keys * cosine + turn(keys) * sine
    k_all[xc] = keys.astype(BF)
    along_x(k_all.at[xc], kxsem, kcsem)
    wpass(V, 2)
    for k in YORDER:
        wuse(V, k)
    v_all[xc] = proj[:, third(V)].astype(BF)
    along_x(v_all.at[xc], vxsem, vcsem)

    for k, d in cross:
        to_y, to_c = lax.rem(y + k, NY), c if d == 0 else other
        src = act_v.at[:, pl.ds(pl.multiple_of(to_y * 1024 + to_c * 512, 512), 512)]
        send(src, actx.at[yc], asem, device(x, to_y, z, to_c))
    lx = pltpu.make_async_copy(
        act_v.at[:, pl.ds(pl.multiple_of(y * 1024 + c * 512, 512), 512)], actx.at[yc], lsem.at[3]
    )
    lx.start()

    arrived(posq.at[pl.ds(0, 7)], psem)
    arrived(posk.at[pl.ds(0, 7)], ksem)
    for kb in range(8):
        poskt[kb] = jnp.broadcast_to(posk[kb].astype(F32), (TOK, TOK)).T
    place_q = jnp.concatenate([posq[i].astype(F32) for i in range(NZ)], 1)
    arrived(og_all.at[pl.ds(0, 7 * TOK)], osem)

    def block_of(step):
        dx, dc = STEPS[step]
        return lax.rem(x - dx + NX, NX) * 2 + (c if dc == 0 else other)

    def relay(buf, sem_x, sem_c):
        for k in (1, 3, 2):
            blk = buf.at[lax.rem(x - k + NX, NX) * 2 + c]
            arrived(blk, sem_x.at[k - 1])
            send(blk, blk, sem_c.at[k], sibling)

    relay(k_all, kxsem, kcsem)
    relay(v_all, vxsem, vcsem)
    arrived(q_all.at[pl.ds(0, 7 * TOK)], qsem)

    def first(step, half):
        kb = block_of(step)
        dx, dc = STEPS[step]
        if half == 0:
            if dc:
                arrived(k_all.at[kb], kcsem.at[dx])
                arrived(v_all.at[kb], vcsem.at[dx])
            kt_all[kb] = k_all[kb].T
        pk = poskt[kb]
        pk = jnp.concatenate([pk, pk], 1)
        for j in (2 * half, 2 * half + 1):
            cols = pl.ds(j * 256, 256)
            s = nt(k_all[kb], q_all[cols, :])
            dp = nt(v_all[kb], og_all[cols, :])
            s = jnp.where(place_q[:, j * 256 : (j + 1) * 256] >= pk, s, LOW)
            top = jnp.max(s, 0, keepdims=True)
            e = jnp.exp2((s - top) * EXP2_SCALE)
            e_all[kb, :, cols] = e
            dp_all[kb, :, cols] = dp
            mb[pl.ds(kb, 1), cols] = top
            lb[pl.ds(kb, 1), cols] = jnp.sum(e, 0, keepdims=True)
            ab[pl.ds(kb, 1), cols] = jnp.sum(e * dp, 0, keepdims=True)

    def stats_send(half):
        cols = pl.ds(half * 512, 512)
        high = mb[:, cols]
        top = jnp.max(high, 0, keepdims=True)
        fade = jnp.exp2((high - top) * EXP2_SCALE)
        total = jnp.sum(lb[:, cols] * fade, 0, keepdims=True)
        st_all[half, z, 0:1, :] = top * EXP2_SCALE + jnp.log2(total)
        st_all[half, z, 1:2, :] = jnp.sum(ab[:, cols] * fade, 0, keepdims=True) / total
        blk = st_all.at[half, z]
        for k in range(1, NZ):
            send(blk, blk, ssem.at[half], zpeer(k))

    def stats_merge(half):
        cols = pl.ds(half * 512, 512)
        arrived(st_all.at[half, pl.ds(0, 7)], ssem.at[half])
        top = st_all[half, 0, 0:1, :]
        for i in range(1, NZ):
            top = jnp.maximum(top, st_all[half, i, 0:1, :])
        total = jnp.zeros((1, 512), F32)
        delta = jnp.zeros((1, 512), F32)
        for i in range(NZ):
            fade = jnp.exp2(st_all[half, i, 0:1, :] - top)
            total += fade
            delta += st_all[half, i, 1:2, :] * fade
        dl[:, cols] = delta / total
        mb[:, cols] = jnp.exp2(mb[:, cols] * EXP2_SCALE - (top + jnp.log2(total)))

    def grads_of(kb, j):
        cols = pl.ds(j * 256, 256)
        p = e_all[kb, :, cols] * mb[pl.ds(kb, 1), cols]
        ds = (p * (dp_all[kb, :, cols] - dl[:, cols])).astype(BF)
        ds_all[rows(kb, TOK), cols] = ds
        return p.astype(BF), ds

    def dq_send(half):
        kt = jnp.concatenate([kt_all[i] for i in range(8)], 1)
        for j in (2 * half, 2 * half + 1):
            dq = nn(kt, ds_all[:, j * 256 : (j + 1) * 256]) * SCALE
            dq_out[2 * j] = dq[:, :TOK].astype(BF)
            dq_out[2 * j + 1] = dq[:, TOK:].astype(BF)
        for to in range(4 * half, 4 * half + 4):

            @pl.when(z != to)
            def _():
                pltpu.make_async_remote_copy(
                    dq_out.at[to], dq_in.at[z], sent, dqsem,
                    device_id=device(x, y, to, c), device_id_type=MESH,
                ).start()

    for step in range(8):
        first(step, 0)
    stats_send(0)
    for step in range(8):
        first(step, 1)
    stats_send(1)
    stats_merge(0)

    for kb in range(8):
        dv = jnp.zeros((TOK, HEAD_DIM), F32)
        dk = jnp.zeros((TOK, HEAD_DIM), F32)
        for j in range(2):
            cols = pl.ds(j * 256, 256)
            p, ds = grads_of(kb, j)
            dv += nn(p, og_all[cols, :])
            dk += nn(ds, q_all[cols, :])
        acc_k[kb] = dk
        acc_v[kb] = dv
    dq_send(0)
    stats_merge(1)
    for kb in range(8):
        for j in range(2, 4):
            p, ds = grads_of(kb, j)
            p_all[kb, :, pl.ds((j - 2) * 256, 256)] = p
    dq_send(1)

    XORDER = (2, 1, 3, 0)

    def value_grad(kb):
        return acc_v[kb] + nn(p_all[kb], og_all[512:, :])

    def key_grad(kb):
        return (acc_k[kb] + nn(ds_all[rows(kb, TOK), 512:], q_all[512:, :])) * SCALE

    def to_sibling(i, grad):
        for k in XORDER:
            dc_out[i, k] = grad(lax.rem(x + k, NX) * 2 + other).astype(BF)
        send(dc_out.at[i], dc_in.at[i], dcsem.at[i], sibling)

    def to_owners(i, own):
        arrived(dc_in.at[i], dcsem.at[i])
        for k in XORDER:
            dx_out[i, k] = (own[k] + dc_in[i, k].astype(F32)).astype(BF)
        for k in XORDER[:3]:
            send(dx_out.at[i, k], dx_in.at[i, k], dxsem.at[i], xpeer(k))

    def collect(i):
        arrived(dx_in.at[i, pl.ds(1, 3)], dxsem.at[i])
        total = dx_out[i, 0].astype(F32)
        for k in range(1, NX):
            total += dx_in[i, k].astype(F32)
        return total

    to_sibling(0, value_grad)
    to_sibling(1, key_grad)
    for k in XORDER:
        acc_own[0, k] = value_grad(lax.rem(x + k, NX) * 2 + c)
    for k in XORDER:
        acc_own[1, k] = key_grad(lax.rem(x + k, NX) * 2 + c)
    to_owners(0, acc_own.at[0])
    to_owners(1, acc_own.at[1])
    lx.wait()
    arrived(actx.at[pl.ds(0, 7)], asem)

    def turn_block(b, carry):
        actxt[:, pl.ds(pl.multiple_of(b * TOK, TOK), TOK)] = actx[b].T
        return carry

    lax.fori_loop(0, 8, turn_block, 0)
    def gp_send(i):
        blk = gp_all.at[yc, :, third(i)]
        for k in (2, 1, 3):
            send(blk, blk, gsem_y.at[i, k - 1], ypeer(k))
        send(blk, blk, gsem_c.at[i], sibling)

    def gp_relay(i):
        for k in YORDER:
            blk = gp_all.at[lax.rem(y - k + NY, NY) * 2 + c, :, third(i)]
            arrived(blk, gsem_y.at[i, k - 1])
            send(blk, blk, gsem_c.at[i], sibling)

    def dw_send(i):
        arrived(gp_all.at[pl.ds(0, 4), :, third(i)], gsem_c.at[i])
        gp = gp_all[:, :, third(i)].reshape(8 * TOK, HEAD_DIM)
        for j in range(NX):
            dwx_out[i, j] = nn(actxt[j * 128 : (j + 1) * 128, :], gp).astype(BF)
        for k in (2, 1, 3):
            to = lax.rem(x + k, NX)
            send(dwx_out.at[i, to], dwx_in.at[i, x], xsem.at[i], xpeer(k))

    def band_send(i):
        arrived(dwx_in.at[i, pl.ds(0, 3)], xsem.at[i])
        dw = dwx_out[i, x].astype(F32)
        for k in range(1, NX):
            dw += dwx_in[i, lax.rem(x + k, NX)].astype(F32)
        dwz_out[i] = dw.astype(BF).reshape(8, 16, HEAD_DIM)
        for k in (4, 3, 5, 2, 6, 1, 7):
            to = lax.rem(z + k, NZ)
            send(dwz_out.at[i, to], dwz_in.at[i, z], zsem.at[i], zpeer(k))

    def band(i, xx, cc):
        return dw_all.at[i, pl.ds(pl.multiple_of(cc * 512 + xx * 128, 128), 128)]

    def piece_send(i):
        arrived(dwz_in.at[i, pl.ds(0, 7)], zsem.at[i])
        dw = dwz_out[i, z].astype(F32)
        for k in range(1, NZ):
            dw += dwz_in[i, lax.rem(z + k, NZ)].astype(F32)
        own = pl.ds(pl.multiple_of(c * 512 + x * 128 + z * 16, 16), 16)
        dw_all[i, own, :] = dw.astype(BF)
        blk = dw_all.at[i, own]
        for k in (4, 3, 5, 2, 6, 1, 7):
            send(blk, blk, zgsem.at[i], zpeer(k))

    def spread(i):
        arrived(dw_all.at[i, pl.ds(0, 7 * 16)], zgsem.at[i])
        blk = band(i, x, c)
        for k in (2, 1, 3):
            send(blk, blk, xgsem.at[i, k - 1], xpeer(k))
        send(blk, blk, sgsem.at[i], sibling)

    def spread_relay(i):
        for k in (1, 3, 2):
            blk = band(i, lax.rem(x - k + NX, NX), c)
            arrived(blk, xgsem.at[i, k - 1])
            send(blk, blk, sgsem.at[i], sibling)

    def finish(i):
        arrived(dw_all.at[i, pl.ds(0, 512)], sgsem.at[i])
        gw_ref[:, third(i)] = dw_all[i].astype(F32)

    gp_all[yc, :, third(2)] = collect(0).astype(BF)
    gp_send(2)
    dkey = collect(1)
    dkey = dkey * cosine - turn(dkey) * sine
    gp_all[yc, :, third(1)] = dkey.astype(BF)
    gp_send(1)
    arrived(dq_in.at[pl.ds(0, 7)], dqsem)
    dq = dq_out[z].astype(F32)
    for k in range(1, NZ):
        dq += dq_in[lax.rem(z + k, NZ)].astype(F32)
    dq = dq.T
    dq = dq * cosine - turn(dq) * sine
    gp_all[yc, :, :HEAD_DIM] = dq.astype(BF)
    gp_send(0)

    def acts_grad(j, carry):
        cols = pl.ds(pl.multiple_of(j * 512, 512), 512)
        ga_ref[0, :, cols] = nt(gp_all[yc], w_v[cols, :])
        return carry

    lax.fori_loop(0, 6, acts_grad, 0)
    gp_relay(2)
    dw_send(2)
    gp_relay(1)
    dw_send(1)
    gp_relay(0)
    dw_send(0)
    band_send(2)
    band_send(1)
    band_send(0)
    piece_send(2)
    lax.fori_loop(6, 8, acts_grad, 0)
    piece_send(1)
    piece_send(0)
    spread(2)
    spread(1)
    spread(0)
    spread_relay(2)
    spread_relay(1)
    finish(2)
    spread_relay(0)
    finish(1)
    finish(0)

    blk = dq_out.at[pl.ds(0, 7)]
    pltpu.make_async_remote_copy(
        blk, blk, sent, dqsem, device_id=sibling, device_id_type=MESH
    ).wait_send()
    for cp in sends:
        cp.wait_send()


def put(ga_ref, gw_ref, ga_hbm, gw_hbm, sem):
    copies = []
    for i in range(2):
        part = pl.ds(i * 64, 64)
        copies.append(pltpu.make_async_copy(ga_ref.at[0, part], ga_hbm.at[0, part], sem.at[0, i]))
        part = pl.ds(i * 512, 512)
        copies.append(pltpu.make_async_copy(gw_ref.at[part], gw_hbm.at[part], sem.at[1, i]))
    for cp in copies:
        cp.start()
    for cp in copies:
        cp.wait()


def shards(activations, weights, positions, out_grad):
    steps = np.arange(HEAD_DIM // 2, dtype=np.float64)
    freq = (ROPE_BASE ** (-(steps * 2.0 / HEAD_DIM))).astype(np.float32)
    freq = jnp.asarray(np.concatenate([freq, freq])[None])
    operands = (freq, activations, weights, positions, out_grad)
    hbm = pl.BlockSpec(memory_space=pltpu.HBM)
    vmem = pl.BlockSpec(memory_space=pltpu.VMEM)
    dma = pltpu.SemaphoreType.DMA
    V = pltpu.VMEM
    scratch = [
        V((1, HEAD_DIM), F32), V((TOK, 4096), BF), V((4096, WIDE), BF), V((1024, HEAD_DIM), BF), V((1024, HEAD_DIM), BF),
        V((NZ, 1, TOK), jnp.int32), V((8, 1, TOK), jnp.int32), V((8, TOK, TOK), F32),
        V((8, TOK, HEAD_DIM), BF), V((8, TOK, HEAD_DIM), BF), V((8, HEAD_DIM, TOK), BF), V((TOK, WIDE), F32),
        V((8, TOK, 1024), F32), V((8, TOK, 1024), F32), V((1024, 1024), BF),
        V((8, 1024), F32), V((8, 1024), F32), V((8, 1024), F32), V((1, 1024), F32),
        V((8, TOK, HEAD_DIM), F32), V((8, TOK, HEAD_DIM), F32), V((8, TOK, 512), BF), V((2, NZ, 2, 512), F32),
        V((NZ, HEAD_DIM, TOK), BF), V((NZ, HEAD_DIM, TOK), BF),
        V((2, NX, TOK, HEAD_DIM), F32), V((2, NX, TOK, HEAD_DIM), BF), V((2, NX, TOK, HEAD_DIM), BF),
        V((2, NX, TOK, HEAD_DIM), BF), V((2, NX, TOK, HEAD_DIM), BF),
        V((8, TOK, WIDE), BF), V((8, TOK, 512), BF), V((512, 1024), BF),
        V((3, NX, 128, 128), BF), V((3, NX, 128, 128), BF), V((8, 128), F32),
        V((3, NZ, 16, 128), BF), V((3, NZ, 16, 128), BF), V((3, 1024, 128), BF),
        dma(()), dma((4,)), dma((3, 3)), dma((3, 3)), dma((3, 3)), dma(()), dma(()), dma(()), dma(()),
        dma((3,)), dma((4,)), dma((3,)), dma((4,)), dma(()), dma((2,)), dma(()), dma((2,)), dma((2,)), dma((3, 3)), dma((3,)), dma((3,)),
        dma((3,)), dma((3,)), dma((3, 3)), dma((3,)),
    ]
    grads = pl.pallas_call(
        kernel,
        out_shape=(pltpu.VMEM((1, TOK, 4096), F32), pltpu.VMEM((1024, WIDE), F32)),
        in_specs=[hbm] * 5,
        out_specs=(vmem, vmem),
        scratch_shapes=scratch,
        compiler_params=pltpu.CompilerParams(
            collective_id=0, has_side_effects=True, vmem_limit_bytes=40 << 20
        ),
    )(*(pltpu.with_memory_space_constraint(a, pltpu.HBM) for a in operands))
    return pl.pallas_call(
        put,
        out_shape=(
            jax.ShapeDtypeStruct((1, TOK, 4096), F32),
            jax.ShapeDtypeStruct((1024, WIDE), F32),
        ),
        in_specs=[vmem, vmem],
        out_specs=(hbm, hbm),
        scratch_shapes=[dma((2, 2))],
        compiler_params=pltpu.CompilerParams(vmem_limit_bytes=8 << 20),
    )(*grads)


def solution(mesh):
    placed = (
        P("dp", ("outer", "inner"), None),
        P("dp", None),
        P("dp", ("outer", "inner")),
        P("dp", ("outer", "inner"), None),
    )
    return jax.shard_map(
        shards,
        mesh=mesh,
        in_specs=placed,
        out_specs=(P("dp", ("outer", "inner"), None), P("dp", None)),
        check_vma=False,
    )
```

```python
import jax
import jax.numpy as jnp
import numpy as np
from jax import lax
from jax.experimental import pallas as pl
from jax.experimental.pallas import tpu as pltpu
from jax.sharding import PartitionSpec as P

HEAD_DIM = 128
ROPE_BASE = 500000.0
NX, NY, NZ, NC = 4, 4, 8, 2
TOK = 128
WIDE = 3 * HEAD_DIM
MESH = pl.DeviceIdType.MESH
BF = jnp.bfloat16
F32 = jnp.float32
SCALE = HEAD_DIM ** (-0.5)
EXP2_SCALE = SCALE * 1.4426950408889634
LOW = -1e30
STEPS = ((0, 0), (0, 1), (1, 0), (3, 0), (2, 0), (1, 1), (3, 1), (2, 1))


def coords():
    outer, inner = lax.axis_index("outer"), lax.axis_index("inner")
    return (
        (outer // 2) * 2 + lax.rem(inner, 2),
        lax.axis_index("dp"),
        inner // 2,
        lax.rem(outer, 2),
    )


def device(x, y, z, c):
    return {"dp": y, "outer": (x // 2) * 2 + c, "inner": z * 2 + lax.rem(x, 2)}


def nt(a, b):
    return lax.dot_general(a, b, (((1,), (1,)), ((), ())), preferred_element_type=F32)


def nn(a, b):
    return lax.dot_general(a, b, (((1,), (0,)), ((), ())), preferred_element_type=F32)


def turn(u):
    lane = lax.broadcasted_iota(jnp.int32, u.shape, 1)
    half = jnp.roll(u, HEAD_DIM // 2, 1) if False else pltpu.roll(u, HEAD_DIM // 2, 1)
    return jnp.where(lane < HEAD_DIM // 2, -half, half)


def kernel(
    freq_hbm, act_hbm, w_hbm, pos_hbm, og_hbm, ga_ref, gw_ref,
    freq_v, act_v, w_v, og_all, q_all, posq, posk, poskt, k_all, v_all, kt_all, proj,
    e_all, dp_all, ds_all, mb, lb, ab, dl, acc_k, acc_v, p_all, st_all,
    dq_out, dq_in, acc_own, dc_out, dc_in, dx_out, dx_in, gp_all, actx, actxt,
    dwx_out, dwx_in, mark, dwz_out, dwz_in, dw_all,
    word, sent, lsem, wsem_y, wsem_x, wsem_c, psem, ksem, osem, qsem, kxsem, kcsem, vxsem, vcsem,
    asem, ssem,
    dqsem, dcsem, dxsem, gsem_y, gsem_c, xsem, zsem, zgsem, xgsem, sgsem,
):
    x, y, z, c = coords()
    other = 1 - c
    xc, yc = x * 2 + c, y * 2 + c
    sends = []

    def xpeer(k):
        return device(lax.rem(x + k, NX), y, z, c)

    def ypeer(k):
        return device(x, lax.rem(y + k, NY), z, c)

    def zpeer(k):
        return device(x, y, lax.rem(z + k, NZ), c)

    sibling = device(x, y, z, other)

    def send(src, dst, rs, dev):
        cp = pltpu.make_async_remote_copy(src, dst, sent, rs, device_id=dev, device_id_type=MESH)
        cp.start()
        sends.append(cp)

    def arrived(dst, rs):
        pltpu.make_async_remote_copy(
            dst, dst, rs, rs, device_id=sibling, device_id_type=MESH
        ).wait_recv()

    def rows(i, n):
        return pl.ds(pl.multiple_of(i * n, n), n)

    cross = [(k, d) for k in range(4) for d in range(2)][1:]

    lw = pltpu.make_async_copy(w_hbm, w_v.at[rows(y, 1024)], lsem.at[0])
    lw.start()
    lp = pltpu.make_async_copy(pos_hbm, posq.at[z], lsem.at[1])
    lp.start()
    lo = pltpu.make_async_copy(og_hbm.at[0], og_all.at[rows(z, TOK)], lsem.at[1])
    lo.start()
    la = pltpu.make_async_copy(act_hbm.at[0], act_v, lsem.at[2])
    la.start()
    lk = pltpu.make_async_copy(pos_hbm, posk.at[xc], lsem.at[1])
    lk.start()
    lf = pltpu.make_async_copy(freq_hbm, freq_v, lsem.at[1])
    lf.start()

    barrier = pltpu.get_barrier_semaphore()
    greet = [sibling, zpeer(1), zpeer(NZ - 1)]
    for k in range(1, 4):
        greet += [xpeer(k), ypeer(k)]
        greet += [
            device(lax.rem(x + k, NX), y, z, other),
            device(x, lax.rem(y + k, NY), z, other),
        ]
    for dev in greet:
        pl.semaphore_signal(barrier, inc=1, device_id=dev, device_id_type=MESH)
    pl.semaphore_wait(barrier, len(greet))

    def third(i):
        return pl.ds(i * HEAD_DIM, HEAD_DIM)

    Q, K, V = range(3)
    YORDER = (1, 3, 2)
    odd = lax.rem(x, 2)
    near, far = odd * 2 + c, (1 - odd) * 2 + c
    near_sib, far_sib = odd * 2 + other, (1 - odd) * 2 + other

    def wblock(owner, piece, cols, start=0, n=256):
        first_row = pl.multiple_of(owner * 1024 + piece * 256 + start, n)
        return w_v.at[pl.ds(first_row, n), cols]

    def wshare(part, k):
        owner, cols = lax.rem(y - k + NY, NY), third(part)
        blk = wblock(owner, near, cols)
        arrived(blk, wsem_y.at[part, k - 1])
        if part != Q and k != 2:
            half = wblock(owner, near, cols, 0 if k == 1 else 128, 128)
            send(half, half, wsem_y.at[part, 1], ypeer(k))
        for i, d in enumerate((1, 3)):
            half = wblock(owner, near, cols, i * 128, 128)
            send(half, half, wsem_x.at[part, k - 1], xpeer(d))
        send(blk, blk, wsem_c.at[part, k - 1], sibling)

    def wpass(part, k):
        owner, cols = lax.rem(y - k + NY, NY), third(part)
        blk = wblock(owner, far, cols)
        arrived(blk, wsem_x.at[part, k - 1])
        send(blk, blk, wsem_c.at[part, k - 1], sibling)

    def wuse(part, k):
        owner, cols = lax.rem(y - k + NY, NY), third(part)
        arrived(w_v.at[pl.ds(0, 512), cols], wsem_c.at[part, k - 1])
        proj[:, cols] += nn(acts(owner), w_v[rows(owner, 1024), cols])

    lw.wait()
    for part in range(3):
        for k in (1, 3) if part else YORDER:
            blk = wblock(y, near, third(part))
            send(blk, blk, wsem_y.at[part, k - 1], ypeer(k))
    def word_send(r):
        for k in (1, NZ - 1):
            pl.semaphore_signal(word.at[r], inc=1, device_id=zpeer(k), device_id_type=MESH)

    word_send(0)
    lo.wait()
    lp.wait()
    lk.wait()
    lf.wait()
    place = posq[z].astype(F32)
    angles = jnp.broadcast_to(place, (TOK, HEAD_DIM)).T * freq_v[...]
    cosine, sine = jnp.cos(angles), jnp.sin(angles)

    la.wait()

    def acts(owner):
        return act_v[:, pl.ds(pl.multiple_of(owner * 1024, 1024), 1024)]

    proj[...] = nn(acts(y), w_v[rows(y, 1024), :])
    def along_x(blk, sem_x, sem_c):
        for k in (2, 1, 3):
            send(blk, blk, sem_x.at[k - 1], xpeer(k))
        send(blk, blk, sem_c.at[0], sibling)

    pl.semaphore_wait(word.at[0], 2)
    word_send(1)
    for k in YORDER:
        wshare(Q, k)
    pl.semaphore_wait(word.at[1], 2)
    word_send(2)
    wshare(K, 1)
    wshare(K, 3)
    pl.semaphore_wait(word.at[2], 2)
    for k in range(1, NZ):
        blk = posq.at[z]
        send(blk, blk, psem, zpeer(k))
    for k, d in cross:
        blk = posk.at[xc]
        dev = device(lax.rem(x + k, NX), y, z, c if d == 0 else other)
        send(blk, blk, ksem, dev)
    for k in range(1, NZ):
        blk = og_all.at[rows(z, TOK)]
        send(blk, blk, osem, zpeer(k))
    wpass(Q, 1)
    wpass(Q, 3)
    wshare(V, 1)
    wshare(V, 3)
    wpass(Q, 2)
    wshare(K, 2)
    for k in YORDER:
        wuse(Q, k)
    queries = proj[:, third(Q)]
    queries = queries * cosine + turn(queries) * sine
    q_all[rows(z, TOK), :] = queries.astype(BF)
    for k in range(1, NZ):
        blk = q_all.at[rows(z, TOK)]
        send(blk, blk, qsem, zpeer(k))
    wshare(V, 2)
    for k in YORDER:
        wpass(K, k)
    wpass(V, 1)
    wpass(V, 3)
    for k in YORDER:
        wuse(K, k)
    keys = proj[:, third(K)]
    keys = keys * cosine + turn(keys) * sine
    k_all[xc] = keys.astype(BF)
    along_x(k_all.at[xc], kxsem, kcsem)
    wpass(V, 2)
    for k in YORDER:
        wuse(V, k)
    v_all[xc] = proj[:, third(V)].astype(BF)
    along_x(v_all.at[xc], vxsem, vcsem)

    for k, d in cross:
        to_y, to_c = lax.rem(y + k, NY), c if d == 0 else other
        src = act_v.at[:, pl.ds(pl.multiple_of(to_y * 1024 + to_c * 512, 512), 512)]
        send(src, actx.at[yc], asem, device(x, to_y, z, to_c))
    lx = pltpu.make_async_copy(
        act_v.at[:, pl.ds(pl.multiple_of(y * 1024 + c * 512, 512), 512)], actx.at[yc], lsem.at[3]
    )
    lx.start()

    arrived(posq.at[pl.ds(0, 7)], psem)
    arrived(posk.at[pl.ds(0, 7)], ksem)
    for kb in range(8):
        poskt[kb] = jnp.broadcast_to(posk[kb].astype(F32), (TOK, TOK)).T
    place_q = jnp.concatenate([posq[i].astype(F32) for i in range(NZ)], 1)
    arrived(og_all.at[pl.ds(0, 7 * TOK)], osem)

    def block_of(step):
        dx, dc = STEPS[step]
        return lax.rem(x - dx + NX, NX) * 2 + (c if dc == 0 else other)

    def relay(buf, sem_x, sem_c):
        for k in (1, 3, 2):
            blk = buf.at[lax.rem(x - k + NX, NX) * 2 + c]
            arrived(blk, sem_x.at[k - 1])
            send(blk, blk, sem_c.at[k], sibling)

    relay(k_all, kxsem, kcsem)
    relay(v_all, vxsem, vcsem)
    arrived(q_all.at[pl.ds(0, 7 * TOK)], qsem)

    def first(step, half):
        kb = block_of(step)
        dx, dc = STEPS[step]
        if half == 0:
            if dc:
                arrived(k_all.at[kb], kcsem.at[dx])
                arrived(v_all.at[kb], vcsem.at[dx])
            kt_all[kb] = k_all[kb].T
        pk = poskt[kb]
        pk = jnp.concatenate([pk, pk], 1)
        for j in (2 * half, 2 * half + 1):
            cols = pl.ds(j * 256, 256)
            s = nt(k_all[kb], q_all[cols, :])
            dp = nt(v_all[kb], og_all[cols, :])
            s = jnp.where(place_q[:, j * 256 : (j + 1) * 256] >= pk, s, LOW)
            top = jnp.max(s, 0, keepdims=True)
            e = jnp.exp2((s - top) * EXP2_SCALE)
            e_all[kb, :, cols] = e
            dp_all[kb, :, cols] = dp
            mb[pl.ds(kb, 1), cols] = top
            lb[pl.ds(kb, 1), cols] = jnp.sum(e, 0, keepdims=True)
            ab[pl.ds(kb, 1), cols] = jnp.sum(e * dp, 0, keepdims=True)

    def stats_send(half):
        cols = pl.ds(half * 512, 512)
        high = mb[:, cols]
        top = jnp.max(high, 0, keepdims=True)
        fade = jnp.exp2((high - top) * EXP2_SCALE)
        total = jnp.sum(lb[:, cols] * fade, 0, keepdims=True)
        st_all[half, z, 0:1, :] = top * EXP2_SCALE + jnp.log2(total)
        st_all[half, z, 1:2, :] = jnp.sum(ab[:, cols] * fade, 0, keepdims=True) / total
        blk = st_all.at[half, z]
        for k in range(1, NZ):
            send(blk, blk, ssem.at[half], zpeer(k))

    def stats_merge(half):
        cols = pl.ds(half * 512, 512)
        arrived(st_all.at[half, pl.ds(0, 7)], ssem.at[half])
        top = st_all[half, 0, 0:1, :]
        for i in range(1, NZ):
            top = jnp.maximum(top, st_all[half, i, 0:1, :])
        total = jnp.zeros((1, 512), F32)
        delta = jnp.zeros((1, 512), F32)
        for i in range(NZ):
            fade = jnp.exp2(st_all[half, i, 0:1, :] - top)
            total += fade
            delta += st_all[half, i, 1:2, :] * fade
        dl[:, cols] = delta / total
        mb[:, cols] = jnp.exp2(mb[:, cols] * EXP2_SCALE - (top + jnp.log2(total)))

    def grads_of(kb, j):
        cols = pl.ds(j * 256, 256)
        p = e_all[kb, :, cols] * mb[pl.ds(kb, 1), cols]
        ds = (p * (dp_all[kb, :, cols] - dl[:, cols])).astype(BF)
        ds_all[rows(kb, TOK), cols] = ds
        return p.astype(BF), ds

    def dq_send(half):
        kt = jnp.concatenate([kt_all[i] for i in range(8)], 1)
        for j in (2 * half, 2 * half + 1):
            dq = nn(kt, ds_all[:, j * 256 : (j + 1) * 256]) * SCALE
            dq_out[2 * j] = dq[:, :TOK].astype(BF)
            dq_out[2 * j + 1] = dq[:, TOK:].astype(BF)
        for to in range(4 * half, 4 * half + 4):

            @pl.when(z != to)
            def _():
                pltpu.make_async_remote_copy(
                    dq_out.at[to], dq_in.at[z], sent, dqsem,
                    device_id=device(x, y, to, c), device_id_type=MESH,
                ).start()

    for step in range(8):
        first(step, 0)
    stats_send(0)
    for step in range(8):
        first(step, 1)
    stats_send(1)
    stats_merge(0)

    for kb in range(8):
        dv = jnp.zeros((TOK, HEAD_DIM), F32)
        dk = jnp.zeros((TOK, HEAD_DIM), F32)
        for j in range(2):
            cols = pl.ds(j * 256, 256)
            p, ds = grads_of(kb, j)
            dv += nn(p, og_all[cols, :])
            dk += nn(ds, q_all[cols, :])
        acc_k[kb] = dk
        acc_v[kb] = dv
    dq_send(0)
    stats_merge(1)
    for kb in range(8):
        for j in range(2, 4):
            p, ds = grads_of(kb, j)
            p_all[kb, :, pl.ds((j - 2) * 256, 256)] = p
    dq_send(1)

    XORDER = (2, 1, 3, 0)

    def value_grad(kb):
        return acc_v[kb] + nn(p_all[kb], og_all[512:, :])

    def key_grad(kb):
        return (acc_k[kb] + nn(ds_all[rows(kb, TOK), 512:], q_all[512:, :])) * SCALE

    def to_sibling(i, grad):
        for k in XORDER:
            dc_out[i, k] = grad(lax.rem(x + k, NX) * 2 + other).astype(BF)
        send(dc_out.at[i], dc_in.at[i], dcsem.at[i], sibling)

    def to_owners(i, own):
        arrived(dc_in.at[i], dcsem.at[i])
        for k in XORDER:
            dx_out[i, k] = (own[k] + dc_in[i, k].astype(F32)).astype(BF)
        for k in XORDER[:3]:
            send(dx_out.at[i, k], dx_in.at[i, k], dxsem.at[i], xpeer(k))

    def collect(i):
        arrived(dx_in.at[i, pl.ds(1, 3)], dxsem.at[i])
        total = dx_out[i, 0].astype(F32)
        for k in range(1, NX):
            total += dx_in[i, k].astype(F32)
        return total

    to_sibling(0, value_grad)
    to_sibling(1, key_grad)
    for k in XORDER:
        acc_own[0, k] = value_grad(lax.rem(x + k, NX) * 2 + c)
    for k in XORDER:
        acc_own[1, k] = key_grad(lax.rem(x + k, NX) * 2 + c)
    to_owners(0, acc_own.at[0])
    to_owners(1, acc_own.at[1])
    lx.wait()
    arrived(actx.at[pl.ds(0, 7)], asem)

    def turn_block(b, carry):
        actxt[:, pl.ds(pl.multiple_of(b * TOK, TOK), TOK)] = actx[b].T
        return carry

    lax.fori_loop(0, 8, turn_block, 0)
    def gp_send(i):
        blk = gp_all.at[yc, :, third(i)]
        for k in (2, 1, 3):
            send(blk, blk, gsem_y.at[i, k - 1], ypeer(k))
        send(blk, blk, gsem_c.at[i], sibling)

    def gp_relay(i):
        for k in YORDER:
            blk = gp_all.at[lax.rem(y - k + NY, NY) * 2 + c, :, third(i)]
            arrived(blk, gsem_y.at[i, k - 1])
            send(blk, blk, gsem_c.at[i], sibling)

    def dw_send(i):
        arrived(gp_all.at[pl.ds(0, 4), :, third(i)], gsem_c.at[i])
        gp = gp_all[:, :, third(i)].reshape(8 * TOK, HEAD_DIM)
        for j in range(NX):
            dwx_out[i, j] = nn(actxt[j * 128 : (j + 1) * 128, :], gp).astype(BF)
        for k in (2, 1, 3):
            to = lax.rem(x + k, NX)
            send(dwx_out.at[i, to], dwx_in.at[i, x], xsem.at[i], xpeer(k))

    def band_send(i):
        arrived(dwx_in.at[i, pl.ds(0, 3)], xsem.at[i])
        dw = dwx_out[i, x].astype(F32)
        for k in range(1, NX):
            dw += dwx_in[i, lax.rem(x + k, NX)].astype(F32)
        dwz_out[i] = dw.astype(BF).reshape(8, 16, HEAD_DIM)
        for k in (4, 3, 5, 2, 6, 1, 7):
            to = lax.rem(z + k, NZ)
            send(dwz_out.at[i, to], dwz_in.at[i, z], zsem.at[i], zpeer(k))

    def band(i, xx, cc):
        return dw_all.at[i, pl.ds(pl.multiple_of(cc * 512 + xx * 128, 128), 128)]

    def piece_send(i):
        arrived(dwz_in.at[i, pl.ds(0, 7)], zsem.at[i])
        dw = dwz_out[i, z].astype(F32)
        for k in range(1, NZ):
            dw += dwz_in[i, lax.rem(z + k, NZ)].astype(F32)
        own = pl.ds(pl.multiple_of(c * 512 + x * 128 + z * 16, 16), 16)
        dw_all[i, own, :] = dw.astype(BF)
        blk = dw_all.at[i, own]
        for k in (4, 3, 5, 2, 6, 1, 7):
            send(blk, blk, zgsem.at[i], zpeer(k))

    def spread(i):
        arrived(dw_all.at[i, pl.ds(0, 7 * 16)], zgsem.at[i])
        blk = band(i, x, c)
        for k in (2, 1, 3):
            send(blk, blk, xgsem.at[i, k - 1], xpeer(k))
        send(blk, blk, sgsem.at[i], sibling)

    def spread_relay(i):
        for k in (1, 3, 2):
            blk = band(i, lax.rem(x - k + NX, NX), c)
            arrived(blk, xgsem.at[i, k - 1])
            send(blk, blk, sgsem.at[i], sibling)

    def finish(i):
        arrived(dw_all.at[i, pl.ds(0, 512)], sgsem.at[i])
        gw_ref[:, third(i)] = dw_all[i].astype(F32)

    gp_all[yc, :, third(2)] = collect(0).astype(BF)
    gp_send(2)
    dkey = collect(1)
    dkey = dkey * cosine - turn(dkey) * sine
    gp_all[yc, :, third(1)] = dkey.astype(BF)
    gp_send(1)
    arrived(dq_in.at[pl.ds(0, 7)], dqsem)
    dq = dq_out[z].astype(F32)
    for k in range(1, NZ):
        dq += dq_in[lax.rem(z + k, NZ)].astype(F32)
    dq = dq.T
    dq = dq * cosine - turn(dq) * sine
    gp_all[yc, :, :HEAD_DIM] = dq.astype(BF)
    gp_send(0)

    def acts_grad(j, carry):
        cols = pl.ds(pl.multiple_of(j * 512, 512), 512)
        ga_ref[0, :, cols] = nt(gp_all[yc], w_v[cols, :])
        return carry

    lax.fori_loop(0, 3, acts_grad, 0)
    gp_relay(2)
    lax.fori_loop(3, 5, acts_grad, 0)
    gp_relay(1)
    dw_send(2)
    gp_relay(0)
    dw_send(1)
    dw_send(0)
    band_send(2)
    band_send(1)
    band_send(0)
    piece_send(2)
    lax.fori_loop(5, 8, acts_grad, 0)
    piece_send(1)
    piece_send(0)
    spread(2)
    spread(1)
    spread(0)
    spread_relay(2)
    spread_relay(1)
    finish(2)
    spread_relay(0)
    finish(1)
    finish(0)

    blk = dq_out.at[pl.ds(0, 7)]
    pltpu.make_async_remote_copy(
        blk, blk, sent, dqsem, device_id=sibling, device_id_type=MESH
    ).wait_send()
    for cp in sends:
        cp.wait_send()


def put(ga_ref, gw_ref, ga_hbm, gw_hbm, sem):
    copies = []
    for i in range(2):
        part = pl.ds(i * 64, 64)
        copies.append(pltpu.make_async_copy(ga_ref.at[0, part], ga_hbm.at[0, part], sem.at[0, i]))
        part = pl.ds(i * 512, 512)
        copies.append(pltpu.make_async_copy(gw_ref.at[part], gw_hbm.at[part], sem.at[1, i]))
    for cp in copies:
        cp.start()
    for cp in copies:
        cp.wait()


def shards(activations, weights, positions, out_grad):
    steps = np.arange(HEAD_DIM // 2, dtype=np.float64)
    freq = (ROPE_BASE ** (-(steps * 2.0 / HEAD_DIM))).astype(np.float32)
    freq = jnp.asarray(np.concatenate([freq, freq])[None])
    operands = (freq, activations, weights, positions, out_grad)
    hbm = pl.BlockSpec(memory_space=pltpu.HBM)
    vmem = pl.BlockSpec(memory_space=pltpu.VMEM)
    dma = pltpu.SemaphoreType.DMA
    V = pltpu.VMEM
    scratch = [
        V((1, HEAD_DIM), F32), V((TOK, 4096), BF), V((4096, WIDE), BF), V((1024, HEAD_DIM), BF), V((1024, HEAD_DIM), BF),
        V((NZ, 1, TOK), jnp.int32), V((8, 1, TOK), jnp.int32), V((8, TOK, TOK), F32),
        V((8, TOK, HEAD_DIM), BF), V((8, TOK, HEAD_DIM), BF), V((8, HEAD_DIM, TOK), BF), V((TOK, WIDE), F32),
        V((8, TOK, 1024), F32), V((8, TOK, 1024), F32), V((1024, 1024), BF),
        V((8, 1024), F32), V((8, 1024), F32), V((8, 1024), F32), V((1, 1024), F32),
        V((8, TOK, HEAD_DIM), F32), V((8, TOK, HEAD_DIM), F32), V((8, TOK, 512), BF), V((2, NZ, 2, 512), F32),
        V((NZ, HEAD_DIM, TOK), BF), V((NZ, HEAD_DIM, TOK), BF),
        V((2, NX, TOK, HEAD_DIM), F32), V((2, NX, TOK, HEAD_DIM), BF), V((2, NX, TOK, HEAD_DIM), BF),
        V((2, NX, TOK, HEAD_DIM), BF), V((2, NX, TOK, HEAD_DIM), BF),
        V((8, TOK, WIDE), BF), V((8, TOK, 512), BF), V((512, 1024), BF),
        V((3, NX, 128, 128), BF), V((3, NX, 128, 128), BF), V((8, 128), F32),
        V((3, NZ, 16, 128), BF), V((3, NZ, 16, 128), BF), V((3, 1024, 128), BF),
        pltpu.SemaphoreType.REGULAR((3,)), dma(()), dma((4,)), dma((3, 3)), dma((3, 3)), dma((3, 3)), dma(()), dma(()), dma(()), dma(()),
        dma((3,)), dma((4,)), dma((3,)), dma((4,)), dma(()), dma((2,)), dma(()), dma((2,)), dma((2,)), dma((3, 3)), dma((3,)), dma((3,)),
        dma((3,)), dma((3,)), dma((3, 3)), dma((3,)),
    ]
    grads = pl.pallas_call(
        kernel,
        out_shape=(pltpu.VMEM((1, TOK, 4096), F32), pltpu.VMEM((1024, WIDE), F32)),
        in_specs=[hbm] * 5,
        out_specs=(vmem, vmem),
        scratch_shapes=scratch,
        compiler_params=pltpu.CompilerParams(
            collective_id=0, has_side_effects=True, vmem_limit_bytes=40 << 20
        ),
    )(*(pltpu.with_memory_space_constraint(a, pltpu.HBM) for a in operands))
    return pl.pallas_call(
        put,
        out_shape=(
            jax.ShapeDtypeStruct((1, TOK, 4096), F32),
            jax.ShapeDtypeStruct((1024, WIDE), F32),
        ),
        in_specs=[vmem, vmem],
        out_specs=(hbm, hbm),
        scratch_shapes=[dma((2, 2))],
        compiler_params=pltpu.CompilerParams(vmem_limit_bytes=8 << 20),
    )(*grads)


def solution(mesh):
    placed = (
        P("dp", ("outer", "inner"), None),
        P("dp", None),
        P("dp", ("outer", "inner")),
        P("dp", ("outer", "inner"), None),
    )
    return jax.shard_map(
        shards,
        mesh=mesh,
        in_specs=placed,
        out_specs=(P("dp", ("outer", "inner"), None), P("dp", None)),
        check_vma=False,
    )
```

```python
import jax
import jax.numpy as jnp
import numpy as np
from jax import lax
from jax.experimental import pallas as pl
from jax.experimental.pallas import tpu as pltpu
from jax.sharding import PartitionSpec as P

HEAD_DIM = 128
ROPE_BASE = 500000.0
NX, NY, NZ, NC = 4, 4, 8, 2
TOK = 128
WIDE = 3 * HEAD_DIM
MESH = pl.DeviceIdType.MESH
BF = jnp.bfloat16
F32 = jnp.float32
SCALE = HEAD_DIM ** (-0.5)
EXP2_SCALE = SCALE * 1.4426950408889634
LOW = -1e30
STEPS = ((0, 0), (0, 1), (1, 0), (3, 0), (2, 0), (1, 1), (3, 1), (2, 1))


def coords():
    outer, inner = lax.axis_index("outer"), lax.axis_index("inner")
    return (
        (outer // 2) * 2 + lax.rem(inner, 2),
        lax.axis_index("dp"),
        inner // 2,
        lax.rem(outer, 2),
    )


def device(x, y, z, c):
    return {"dp": y, "outer": (x // 2) * 2 + c, "inner": z * 2 + lax.rem(x, 2)}


def nt(a, b):
    return lax.dot_general(a, b, (((1,), (1,)), ((), ())), preferred_element_type=F32)


def nn(a, b):
    return lax.dot_general(a, b, (((1,), (0,)), ((), ())), preferred_element_type=F32)


def turn(u):
    lane = lax.broadcasted_iota(jnp.int32, u.shape, 1)
    half = jnp.roll(u, HEAD_DIM // 2, 1) if False else pltpu.roll(u, HEAD_DIM // 2, 1)
    return jnp.where(lane < HEAD_DIM // 2, -half, half)


def kernel(
    freq_hbm, act_hbm, w_hbm, pos_hbm, og_hbm, ga_ref, gw_ref,
    freq_v, act_v, w_v, og_all, q_all, posq, posk, poskt, k_all, v_all, kt_all, proj,
    e_all, dp_all, ds_all, mb, lb, ab, dl, acc_k, acc_v, p_all, st_all,
    dq_out, dq_in, acc_own, dc_out, dc_in, dx_out, dx_in, gp_all, actx, actxt,
    dwx_out, dwx_in, mark, dwz_out, dwz_in, dw_all,
    word, sent, lsem, wsem_y, wsem_x, wsem_c, psem, ksem, osem, qsem, kxsem, kcsem, vxsem, vcsem,
    asem, ssem,
    dqsem, dcsem, dxsem, gsem_y, gsem_c, xsem, zsem, zgsem, xgsem, sgsem,
):
    x, y, z, c = coords()
    other = 1 - c
    xc, yc = x * 2 + c, y * 2 + c
    sends = []

    def xpeer(k):
        return device(lax.rem(x + k, NX), y, z, c)

    def ypeer(k):
        return device(x, lax.rem(y + k, NY), z, c)

    def zpeer(k):
        return device(x, y, lax.rem(z + k, NZ), c)

    sibling = device(x, y, z, other)

    def send(src, dst, rs, dev):
        cp = pltpu.make_async_remote_copy(src, dst, sent, rs, device_id=dev, device_id_type=MESH)
        cp.start()
        sends.append(cp)

    def arrived(dst, rs):
        pltpu.make_async_remote_copy(
            dst, dst, rs, rs, device_id=sibling, device_id_type=MESH
        ).wait_recv()

    def rows(i, n):
        return pl.ds(pl.multiple_of(i * n, n), n)

    cross = [(k, d) for k in range(4) for d in range(2)][1:]

    lw = pltpu.make_async_copy(w_hbm, w_v.at[rows(y, 1024)], lsem.at[0])
    lw.start()
    lp = pltpu.make_async_copy(pos_hbm, posq.at[z], lsem.at[1])
    lp.start()
    lo = pltpu.make_async_copy(og_hbm.at[0], og_all.at[rows(z, TOK)], lsem.at[1])
    lo.start()
    la = pltpu.make_async_copy(act_hbm.at[0], act_v, lsem.at[2])
    la.start()
    lk = pltpu.make_async_copy(pos_hbm, posk.at[xc], lsem.at[1])
    lk.start()
    lf = pltpu.make_async_copy(freq_hbm, freq_v, lsem.at[1])
    lf.start()

    barrier = pltpu.get_barrier_semaphore()
    greet = [sibling, zpeer(1), zpeer(NZ - 1)]
    for k in range(1, 4):
        greet += [xpeer(k), ypeer(k)]
        greet += [
            device(lax.rem(x + k, NX), y, z, other),
            device(x, lax.rem(y + k, NY), z, other),
        ]
    for dev in greet:
        pl.semaphore_signal(barrier, inc=1, device_id=dev, device_id_type=MESH)
    pl.semaphore_wait(barrier, len(greet))

    def third(i):
        return pl.ds(i * HEAD_DIM, HEAD_DIM)

    Q, K, V = range(3)
    YORDER = (1, 3, 2)
    odd = lax.rem(x, 2)
    near, far = odd * 2 + c, (1 - odd) * 2 + c
    near_sib, far_sib = odd * 2 + other, (1 - odd) * 2 + other

    def wblock(owner, piece, cols, start=0, n=256):
        first_row = pl.multiple_of(owner * 1024 + piece * 256 + start, n)
        return w_v.at[pl.ds(first_row, n), cols]

    def wshare(part, k):
        owner, cols = lax.rem(y - k + NY, NY), third(part)
        blk = wblock(owner, near, cols)
        arrived(blk, wsem_y.at[part, k - 1])
        if part != Q and k != 2:
            half = wblock(owner, near, cols, 0 if k == 1 else 128, 128)
            send(half, half, wsem_y.at[part, 1], ypeer(k))
        for i, d in enumerate((1, 3)):
            half = wblock(owner, near, cols, i * 128, 128)
            send(half, half, wsem_x.at[part, k - 1], xpeer(d))
        send(blk, blk, wsem_c.at[part, k - 1], sibling)

    def wpass(part, k):
        owner, cols = lax.rem(y - k + NY, NY), third(part)
        blk = wblock(owner, far, cols)
        arrived(blk, wsem_x.at[part, k - 1])
        send(blk, blk, wsem_c.at[part, k - 1], sibling)

    def wuse(part, k):
        owner, cols = lax.rem(y - k + NY, NY), third(part)
        arrived(w_v.at[pl.ds(0, 512), cols], wsem_c.at[part, k - 1])
        proj[:, cols] += nn(acts(owner), w_v[rows(owner, 1024), cols])

    lw.wait()
    for part in range(3):
        for k in (1, 3) if part else YORDER:
            blk = wblock(y, near, third(part))
            send(blk, blk, wsem_y.at[part, k - 1], ypeer(k))
    def word_send(r):
        for k in (1, NZ - 1):
            pl.semaphore_signal(word.at[r], inc=1, device_id=zpeer(k), device_id_type=MESH)

    word_send(0)
    lo.wait()
    lp.wait()
    lk.wait()
    lf.wait()
    place = posq[z].astype(F32)
    angles = jnp.broadcast_to(place, (TOK, HEAD_DIM)).T * freq_v[...]
    cosine, sine = jnp.cos(angles), jnp.sin(angles)

    la.wait()

    def acts(owner):
        return act_v[:, pl.ds(pl.multiple_of(owner * 1024, 1024), 1024)]

    proj[...] = nn(acts(y), w_v[rows(y, 1024), :])
    def along_x(blk, sem_x, sem_c):
        for k in (2, 1, 3):
            send(blk, blk, sem_x.at[k - 1], xpeer(k))
        send(blk, blk, sem_c.at[0], sibling)

    pl.semaphore_wait(word.at[0], 2)
    word_send(1)
    for k in YORDER:
        wshare(Q, k)
    pl.semaphore_wait(word.at[1], 2)
    word_send(2)
    wshare(K, 1)
    wshare(K, 3)
    pl.semaphore_wait(word.at[2], 2)
    for k in range(1, NZ):
        blk = posq.at[z]
        send(blk, blk, psem, zpeer(k))
    for k, d in cross:
        blk = posk.at[xc]
        dev = device(lax.rem(x + k, NX), y, z, c if d == 0 else other)
        send(blk, blk, ksem, dev)
    for k in range(1, NZ):
        blk = og_all.at[rows(z, TOK)]
        send(blk, blk, osem, zpeer(k))
    wpass(Q, 1)
    wpass(Q, 3)
    wshare(V, 1)
    wshare(V, 3)
    wpass(Q, 2)
    wshare(K, 2)
    for k in YORDER:
        wuse(Q, k)
    queries = proj[:, third(Q)]
    queries = queries * cosine + turn(queries) * sine
    q_all[rows(z, TOK), :] = queries.astype(BF)
    for k in (4, 3, 5, 2, 6, 1, 7):
        blk = q_all.at[rows(z, TOK)]
        send(blk, blk, qsem, zpeer(k))
    wshare(V, 2)
    for k in YORDER:
        wpass(K, k)
    wpass(V, 1)
    wpass(V, 3)
    for k in YORDER:
        wuse(K, k)
    keys = proj[:, third(K)]
    keys = keys * cosine + turn(keys) * sine
    k_all[xc] = keys.astype(BF)
    along_x(k_all.at[xc], kxsem, kcsem)
    wpass(V, 2)
    for k in YORDER:
        wuse(V, k)
    v_all[xc] = proj[:, third(V)].astype(BF)
    along_x(v_all.at[xc], vxsem, vcsem)

    for k, d in cross:
        to_y, to_c = lax.rem(y + k, NY), c if d == 0 else other
        src = act_v.at[:, pl.ds(pl.multiple_of(to_y * 1024 + to_c * 512, 512), 512)]
        send(src, actx.at[yc], asem, device(x, to_y, z, to_c))
    lx = pltpu.make_async_copy(
        act_v.at[:, pl.ds(pl.multiple_of(y * 1024 + c * 512, 512), 512)], actx.at[yc], lsem.at[3]
    )
    lx.start()

    arrived(posq.at[pl.ds(0, 7)], psem)
    arrived(posk.at[pl.ds(0, 7)], ksem)
    for kb in range(8):
        poskt[kb] = jnp.broadcast_to(posk[kb].astype(F32), (TOK, TOK)).T
    place_q = jnp.concatenate([posq[i].astype(F32) for i in range(NZ)], 1)
    arrived(og_all.at[pl.ds(0, 7 * TOK)], osem)

    def block_of(step):
        dx, dc = STEPS[step]
        return lax.rem(x - dx + NX, NX) * 2 + (c if dc == 0 else other)

    def relay(buf, sem_x, sem_c):
        for k in (1, 3, 2):
            blk = buf.at[lax.rem(x - k + NX, NX) * 2 + c]
            arrived(blk, sem_x.at[k - 1])
            send(blk, blk, sem_c.at[k], sibling)

    relay(k_all, kxsem, kcsem)
    relay(v_all, vxsem, vcsem)
    arrived(q_all.at[pl.ds(0, 7 * TOK)], qsem)

    def first(step, half):
        kb = block_of(step)
        dx, dc = STEPS[step]
        if half == 0:
            if dc:
                arrived(k_all.at[kb], kcsem.at[dx])
                arrived(v_all.at[kb], vcsem.at[dx])
            kt_all[kb] = k_all[kb].T
        pk = poskt[kb]
        pk = jnp.concatenate([pk, pk], 1)
        for j in (2 * half, 2 * half + 1):
            cols = pl.ds(j * 256, 256)
            s = nt(k_all[kb], q_all[cols, :])
            dp = nt(v_all[kb], og_all[cols, :])
            s = jnp.where(place_q[:, j * 256 : (j + 1) * 256] >= pk, s, LOW)
            top = jnp.max(s, 0, keepdims=True)
            e = jnp.exp2((s - top) * EXP2_SCALE)
            e_all[kb, :, cols] = e
            dp_all[kb, :, cols] = dp
            mb[pl.ds(kb, 1), cols] = top
            lb[pl.ds(kb, 1), cols] = jnp.sum(e, 0, keepdims=True)
            ab[pl.ds(kb, 1), cols] = jnp.sum(e * dp, 0, keepdims=True)

    def stats_send(half):
        cols = pl.ds(half * 512, 512)
        high = mb[:, cols]
        top = jnp.max(high, 0, keepdims=True)
        fade = jnp.exp2((high - top) * EXP2_SCALE)
        total = jnp.sum(lb[:, cols] * fade, 0, keepdims=True)
        st_all[half, z, 0:1, :] = top * EXP2_SCALE + jnp.log2(total)
        st_all[half, z, 1:2, :] = jnp.sum(ab[:, cols] * fade, 0, keepdims=True) / total
        blk = st_all.at[half, z]
        for k in (4, 3, 5, 2, 6, 1, 7):
            send(blk, blk, ssem.at[half], zpeer(k))

    def stats_merge(half):
        cols = pl.ds(half * 512, 512)
        arrived(st_all.at[half, pl.ds(0, 7)], ssem.at[half])
        top = st_all[half, 0, 0:1, :]
        for i in range(1, NZ):
            top = jnp.maximum(top, st_all[half, i, 0:1, :])
        total = jnp.zeros((1, 512), F32)
        delta = jnp.zeros((1, 512), F32)
        for i in range(NZ):
            fade = jnp.exp2(st_all[half, i, 0:1, :] - top)
            total += fade
            delta += st_all[half, i, 1:2, :] * fade
        dl[:, cols] = delta / total
        mb[:, cols] = jnp.exp2(mb[:, cols] * EXP2_SCALE - (top + jnp.log2(total)))

    def grads_of(kb, j):
        cols = pl.ds(j * 256, 256)
        p = e_all[kb, :, cols] * mb[pl.ds(kb, 1), cols]
        ds = (p * (dp_all[kb, :, cols] - dl[:, cols])).astype(BF)
        ds_all[rows(kb, TOK), cols] = ds
        return p.astype(BF), ds

    def dq_send(half):
        kt = jnp.concatenate([kt_all[i] for i in range(8)], 1)
        for j in (2 * half, 2 * half + 1):
            dq = nn(kt, ds_all[:, j * 256 : (j + 1) * 256]) * SCALE
            dq_out[2 * j] = dq[:, :TOK].astype(BF)
            dq_out[2 * j + 1] = dq[:, TOK:].astype(BF)
        for k in (4, 3, 5, 2, 6, 1, 7):
            to = lax.rem(z + k, NZ)

            @pl.when(to // 4 == half)
            def _():
                pltpu.make_async_remote_copy(
                    dq_out.at[to], dq_in.at[z], sent, dqsem,
                    device_id=zpeer(k), device_id_type=MESH,
                ).start()

    for step in range(8):
        first(step, 0)
    stats_send(0)
    for step in range(8):
        first(step, 1)
    stats_send(1)
    stats_merge(0)

    for kb in range(8):
        dv = jnp.zeros((TOK, HEAD_DIM), F32)
        dk = jnp.zeros((TOK, HEAD_DIM), F32)
        for j in range(2):
            cols = pl.ds(j * 256, 256)
            p, ds = grads_of(kb, j)
            dv += nn(p, og_all[cols, :])
            dk += nn(ds, q_all[cols, :])
        acc_k[kb] = dk
        acc_v[kb] = dv
    dq_send(0)
    stats_merge(1)
    for kb in range(8):
        for j in range(2, 4):
            p, ds = grads_of(kb, j)
            p_all[kb, :, pl.ds((j - 2) * 256, 256)] = p
    dq_send(1)

    XORDER = (2, 1, 3, 0)

    def value_grad(kb):
        return acc_v[kb] + nn(p_all[kb], og_all[512:, :])

    def key_grad(kb):
        return (acc_k[kb] + nn(ds_all[rows(kb, TOK), 512:], q_all[512:, :])) * SCALE

    def to_sibling(i, grad):
        for k in XORDER:
            dc_out[i, k] = grad(lax.rem(x + k, NX) * 2 + other).astype(BF)
        send(dc_out.at[i], dc_in.at[i], dcsem.at[i], sibling)

    def to_owners(i, own):
        arrived(dc_in.at[i], dcsem.at[i])
        for k in XORDER:
            dx_out[i, k] = (own[k] + dc_in[i, k].astype(F32)).astype(BF)
        for k in XORDER[:3]:
            send(dx_out.at[i, k], dx_in.at[i, k], dxsem.at[i], xpeer(k))

    def collect(i):
        arrived(dx_in.at[i, pl.ds(1, 3)], dxsem.at[i])
        total = dx_out[i, 0].astype(F32)
        for k in range(1, NX):
            total += dx_in[i, k].astype(F32)
        return total

    to_sibling(0, value_grad)
    to_sibling(1, key_grad)
    for k in XORDER:
        acc_own[0, k] = value_grad(lax.rem(x + k, NX) * 2 + c)
    for k in XORDER:
        acc_own[1, k] = key_grad(lax.rem(x + k, NX) * 2 + c)
    to_owners(0, acc_own.at[0])
    to_owners(1, acc_own.at[1])
    lx.wait()
    arrived(actx.at[pl.ds(0, 7)], asem)

    def turn_block(b, carry):
        actxt[:, pl.ds(pl.multiple_of(b * TOK, TOK), TOK)] = actx[b].T
        return carry

    lax.fori_loop(0, 8, turn_block, 0)
    def gp_send(i):
        blk = gp_all.at[yc, :, third(i)]
        for k in (2, 1, 3):
            send(blk, blk, gsem_y.at[i, k - 1], ypeer(k))
        send(blk, blk, gsem_c.at[i], sibling)

    def gp_relay(i):
        for k in YORDER:
            blk = gp_all.at[lax.rem(y - k + NY, NY) * 2 + c, :, third(i)]
            arrived(blk, gsem_y.at[i, k - 1])
            send(blk, blk, gsem_c.at[i], sibling)

    def dw_send(i):
        arrived(gp_all.at[pl.ds(0, 4), :, third(i)], gsem_c.at[i])
        gp = gp_all[:, :, third(i)].reshape(8 * TOK, HEAD_DIM)
        for j in range(NX):
            dwx_out[i, j] = nn(actxt[j * 128 : (j + 1) * 128, :], gp).astype(BF)
        for k in (2, 1, 3):
            to = lax.rem(x + k, NX)
            send(dwx_out.at[i, to], dwx_in.at[i, x], xsem.at[i], xpeer(k))

    def band_send(i):
        arrived(dwx_in.at[i, pl.ds(0, 3)], xsem.at[i])
        dw = dwx_out[i, x].astype(F32)
        for k in range(1, NX):
            dw += dwx_in[i, lax.rem(x + k, NX)].astype(F32)
        dwz_out[i] = dw.astype(BF).reshape(8, 16, HEAD_DIM)
        for k in (4, 3, 5, 2, 6, 1, 7):
            to = lax.rem(z + k, NZ)
            send(dwz_out.at[i, to], dwz_in.at[i, z], zsem.at[i], zpeer(k))

    def band(i, xx, cc):
        return dw_all.at[i, pl.ds(pl.multiple_of(cc * 512 + xx * 128, 128), 128)]

    def piece_send(i):
        arrived(dwz_in.at[i, pl.ds(0, 7)], zsem.at[i])
        dw = dwz_out[i, z].astype(F32)
        for k in range(1, NZ):
            dw += dwz_in[i, lax.rem(z + k, NZ)].astype(F32)
        own = pl.ds(pl.multiple_of(c * 512 + x * 128 + z * 16, 16), 16)
        dw_all[i, own, :] = dw.astype(BF)
        blk = dw_all.at[i, own]
        for k in (4, 3, 5, 2, 6, 1, 7):
            send(blk, blk, zgsem.at[i], zpeer(k))

    def spread(i):
        arrived(dw_all.at[i, pl.ds(0, 7 * 16)], zgsem.at[i])
        blk = band(i, x, c)
        for k in (2, 1, 3):
            send(blk, blk, xgsem.at[i, k - 1], xpeer(k))
        send(blk, blk, sgsem.at[i], sibling)

    def spread_relay(i):
        for k in (1, 3, 2):
            blk = band(i, lax.rem(x - k + NX, NX), c)
            arrived(blk, xgsem.at[i, k - 1])
            send(blk, blk, sgsem.at[i], sibling)

    def finish(i):
        arrived(dw_all.at[i, pl.ds(0, 512)], sgsem.at[i])
        gw_ref[:, third(i)] = dw_all[i].astype(F32)

    gp_all[yc, :, third(2)] = collect(0).astype(BF)
    gp_send(2)
    dkey = collect(1)
    dkey = dkey * cosine - turn(dkey) * sine
    gp_all[yc, :, third(1)] = dkey.astype(BF)
    gp_send(1)
    arrived(dq_in.at[pl.ds(0, 7)], dqsem)
    dq = dq_out[z].astype(F32)
    for k in range(1, NZ):
        dq += dq_in[lax.rem(z + k, NZ)].astype(F32)
    dq = dq.T
    dq = dq * cosine - turn(dq) * sine
    gp_all[yc, :, :HEAD_DIM] = dq.astype(BF)
    gp_send(0)

    def acts_grad(j, carry):
        cols = pl.ds(pl.multiple_of(j * 512, 512), 512)
        ga_ref[0, :, cols] = nt(gp_all[yc], w_v[cols, :])
        return carry

    lax.fori_loop(0, 3, acts_grad, 0)
    gp_relay(2)
    lax.fori_loop(3, 5, acts_grad, 0)
    gp_relay(1)
    dw_send(2)
    gp_relay(0)
    dw_send(1)
    dw_send(0)
    band_send(2)
    band_send(1)
    band_send(0)
    piece_send(2)
    lax.fori_loop(5, 8, acts_grad, 0)
    piece_send(1)
    piece_send(0)
    spread(2)
    spread(1)
    spread(0)
    spread_relay(2)
    spread_relay(1)
    finish(2)
    spread_relay(0)
    finish(1)
    finish(0)

    blk = dq_out.at[pl.ds(0, 7)]
    pltpu.make_async_remote_copy(
        blk, blk, sent, dqsem, device_id=sibling, device_id_type=MESH
    ).wait_send()
    for cp in sends:
        cp.wait_send()


def put(ga_ref, gw_ref, ga_hbm, gw_hbm, sem):
    copies = []
    for i in range(2):
        part = pl.ds(i * 64, 64)
        copies.append(pltpu.make_async_copy(ga_ref.at[0, part], ga_hbm.at[0, part], sem.at[0, i]))
        part = pl.ds(i * 512, 512)
        copies.append(pltpu.make_async_copy(gw_ref.at[part], gw_hbm.at[part], sem.at[1, i]))
    for cp in copies:
        cp.start()
    for cp in copies:
        cp.wait()


def shards(activations, weights, positions, out_grad):
    steps = np.arange(HEAD_DIM // 2, dtype=np.float64)
    freq = (ROPE_BASE ** (-(steps * 2.0 / HEAD_DIM))).astype(np.float32)
    freq = jnp.asarray(np.concatenate([freq, freq])[None])
    operands = (freq, activations, weights, positions, out_grad)
    hbm = pl.BlockSpec(memory_space=pltpu.HBM)
    vmem = pl.BlockSpec(memory_space=pltpu.VMEM)
    dma = pltpu.SemaphoreType.DMA
    V = pltpu.VMEM
    scratch = [
        V((1, HEAD_DIM), F32), V((TOK, 4096), BF), V((4096, WIDE), BF), V((1024, HEAD_DIM), BF), V((1024, HEAD_DIM), BF),
        V((NZ, 1, TOK), jnp.int32), V((8, 1, TOK), jnp.int32), V((8, TOK, TOK), F32),
        V((8, TOK, HEAD_DIM), BF), V((8, TOK, HEAD_DIM), BF), V((8, HEAD_DIM, TOK), BF), V((TOK, WIDE), F32),
        V((8, TOK, 1024), F32), V((8, TOK, 1024), F32), V((1024, 1024), BF),
        V((8, 1024), F32), V((8, 1024), F32), V((8, 1024), F32), V((1, 1024), F32),
        V((8, TOK, HEAD_DIM), F32), V((8, TOK, HEAD_DIM), F32), V((8, TOK, 512), BF), V((2, NZ, 2, 512), F32),
        V((NZ, HEAD_DIM, TOK), BF), V((NZ, HEAD_DIM, TOK), BF),
        V((2, NX, TOK, HEAD_DIM), F32), V((2, NX, TOK, HEAD_DIM), BF), V((2, NX, TOK, HEAD_DIM), BF),
        V((2, NX, TOK, HEAD_DIM), BF), V((2, NX, TOK, HEAD_DIM), BF),
        V((8, TOK, WIDE), BF), V((8, TOK, 512), BF), V((512, 1024), BF),
        V((3, NX, 128, 128), BF), V((3, NX, 128, 128), BF), V((8, 128), F32),
        V((3, NZ, 16, 128), BF), V((3, NZ, 16, 128), BF), V((3, 1024, 128), BF),
        pltpu.SemaphoreType.REGULAR((3,)), dma(()), dma((4,)), dma((3, 3)), dma((3, 3)), dma((3, 3)), dma(()), dma(()), dma(()), dma(()),
        dma((3,)), dma((4,)), dma((3,)), dma((4,)), dma(()), dma((2,)), dma(()), dma((2,)), dma((2,)), dma((3, 3)), dma((3,)), dma((3,)),
        dma((3,)), dma((3,)), dma((3, 3)), dma((3,)),
    ]
    grads = pl.pallas_call(
        kernel,
        out_shape=(pltpu.VMEM((1, TOK, 4096), F32), pltpu.VMEM((1024, WIDE), F32)),
        in_specs=[hbm] * 5,
        out_specs=(vmem, vmem),
        scratch_shapes=scratch,
        compiler_params=pltpu.CompilerParams(
            collective_id=0, has_side_effects=True, vmem_limit_bytes=40 << 20
        ),
    )(*(pltpu.with_memory_space_constraint(a, pltpu.HBM) for a in operands))
    return pl.pallas_call(
        put,
        out_shape=(
            jax.ShapeDtypeStruct((1, TOK, 4096), F32),
            jax.ShapeDtypeStruct((1024, WIDE), F32),
        ),
        in_specs=[vmem, vmem],
        out_specs=(hbm, hbm),
        scratch_shapes=[dma((2, 2))],
        compiler_params=pltpu.CompilerParams(vmem_limit_bytes=8 << 20),
    )(*grads)


def solution(mesh):
    placed = (
        P("dp", ("outer", "inner"), None),
        P("dp", None),
        P("dp", ("outer", "inner")),
        P("dp", ("outer", "inner"), None),
    )
    return jax.shard_map(
        shards,
        mesh=mesh,
        in_specs=placed,
        out_specs=(P("dp", ("outer", "inner"), None), P("dp", None)),
        check_vma=False,
    )
```

```python
import jax
import jax.numpy as jnp
import numpy as np
from jax import lax
from jax.experimental import pallas as pl
from jax.experimental.pallas import tpu as pltpu
from jax.sharding import PartitionSpec as P

HEAD_DIM = 128
ROPE_BASE = 500000.0
NX, NY, NZ, NC = 4, 4, 8, 2
TOK = 128
WIDE = 3 * HEAD_DIM
MESH = pl.DeviceIdType.MESH
BF = jnp.bfloat16
F32 = jnp.float32
SCALE = HEAD_DIM ** (-0.5)
EXP2_SCALE = SCALE * 1.4426950408889634
LOW = -1e30
STEPS = ((0, 0), (0, 1), (1, 0), (3, 0), (2, 0), (1, 1), (3, 1), (2, 1))


def coords():
    outer, inner = lax.axis_index("outer"), lax.axis_index("inner")
    return (
        (outer // 2) * 2 + lax.rem(inner, 2),
        lax.axis_index("dp"),
        inner // 2,
        lax.rem(outer, 2),
    )


def device(x, y, z, c):
    return {"dp": y, "outer": (x // 2) * 2 + c, "inner": z * 2 + lax.rem(x, 2)}


def nt(a, b):
    return lax.dot_general(a, b, (((1,), (1,)), ((), ())), preferred_element_type=F32)


def nn(a, b):
    return lax.dot_general(a, b, (((1,), (0,)), ((), ())), preferred_element_type=F32)


def turn(u):
    lane = lax.broadcasted_iota(jnp.int32, u.shape, 1)
    half = jnp.roll(u, HEAD_DIM // 2, 1) if False else pltpu.roll(u, HEAD_DIM // 2, 1)
    return jnp.where(lane < HEAD_DIM // 2, -half, half)


def kernel(
    freq_hbm, act_hbm, w_hbm, pos_hbm, og_hbm, ga_ref, gw_ref,
    freq_v, act_v, w_v, og_all, q_all, posq, posk, poskt, k_all, v_all, kt_all, proj,
    e_all, dp_all, ds_all, mb, lb, ab, dl, acc_k, acc_v, p_all, st_all,
    dq_out, dq_in, acc_own, dc_out, dc_in, dx_out, dx_in, gp_all, actx, actxt,
    dwx_out, dwx_in, mark, dwz_out, dwz_in, dw_all,
    word, sent, lsem, wsem_y, wsem_x, wsem_c, psem, ksem, osem, qsem, kxsem, kcsem, vxsem, vcsem,
    asem, ssem,
    dqsem, dcsem, dxsem, gsem_y, gsem_c, xsem, zsem, zgsem, xgsem, sgsem,
):
    x, y, z, c = coords()
    other = 1 - c
    xc, yc = x * 2 + c, y * 2 + c
    sends = []

    def xpeer(k):
        return device(lax.rem(x + k, NX), y, z, c)

    def ypeer(k):
        return device(x, lax.rem(y + k, NY), z, c)

    def zpeer(k):
        return device(x, y, lax.rem(z + k, NZ), c)

    sibling = device(x, y, z, other)

    def send(src, dst, rs, dev):
        cp = pltpu.make_async_remote_copy(src, dst, sent, rs, device_id=dev, device_id_type=MESH)
        cp.start()
        sends.append(cp)

    def arrived(dst, rs):
        pltpu.make_async_remote_copy(
            dst, dst, rs, rs, device_id=sibling, device_id_type=MESH
        ).wait_recv()

    def rows(i, n):
        return pl.ds(pl.multiple_of(i * n, n), n)

    cross = [(k, d) for k in range(4) for d in range(2)][1:]

    lw = pltpu.make_async_copy(w_hbm, w_v.at[rows(y, 1024)], lsem.at[0])
    lw.start()
    lp = pltpu.make_async_copy(pos_hbm, posq.at[z], lsem.at[1])
    lp.start()
    lo = pltpu.make_async_copy(og_hbm.at[0], og_all.at[rows(z, TOK)], lsem.at[1])
    lo.start()
    la = pltpu.make_async_copy(act_hbm.at[0], act_v, lsem.at[2])
    la.start()
    lk = pltpu.make_async_copy(pos_hbm, posk.at[xc], lsem.at[1])
    lk.start()
    lf = pltpu.make_async_copy(freq_hbm, freq_v, lsem.at[1])
    lf.start()

    barrier = pltpu.get_barrier_semaphore()
    greet = [sibling, zpeer(1), zpeer(NZ - 1)]
    for k in range(1, 4):
        greet += [xpeer(k), ypeer(k)]
        greet += [
            device(lax.rem(x + k, NX), y, z, other),
            device(x, lax.rem(y + k, NY), z, other),
        ]
    for dev in greet:
        pl.semaphore_signal(barrier, inc=1, device_id=dev, device_id_type=MESH)
    pl.semaphore_wait(barrier, len(greet))

    def third(i):
        return pl.ds(i * HEAD_DIM, HEAD_DIM)

    Q, K, V = range(3)
    YORDER = (1, 3, 2)
    odd = lax.rem(x, 2)
    near, far = odd * 2 + c, (1 - odd) * 2 + c
    near_sib, far_sib = odd * 2 + other, (1 - odd) * 2 + other

    def wblock(owner, piece, cols, start=0, n=256):
        first_row = pl.multiple_of(owner * 1024 + piece * 256 + start, n)
        return w_v.at[pl.ds(first_row, n), cols]

    def wshare(part, k):
        owner, cols = lax.rem(y - k + NY, NY), third(part)
        blk = wblock(owner, near, cols)
        arrived(blk, wsem_y.at[part, k - 1])
        if part != Q and k != 2:
            half = wblock(owner, near, cols, 0 if k == 1 else 128, 128)
            send(half, half, wsem_y.at[part, 1], ypeer(k))
        for i, d in enumerate((1, 3)):
            half = wblock(owner, near, cols, i * 128, 128)
            send(half, half, wsem_x.at[part, k - 1], xpeer(d))
        send(blk, blk, wsem_c.at[part, k - 1], sibling)

    def wpass(part, k):
        owner, cols = lax.rem(y - k + NY, NY), third(part)
        blk = wblock(owner, far, cols)
        arrived(blk, wsem_x.at[part, k - 1])
        send(blk, blk, wsem_c.at[part, k - 1], sibling)

    def wuse(part, k):
        owner, cols = lax.rem(y - k + NY, NY), third(part)
        arrived(w_v.at[pl.ds(0, 512), cols], wsem_c.at[part, k - 1])
        proj[:, cols] += nn(acts(owner), w_v[rows(owner, 1024), cols])

    lw.wait()
    for part in range(3):
        for k in (1, 3) if part else (2, 1, 3):
            blk = wblock(y, near, third(part))
            send(blk, blk, wsem_y.at[part, k - 1], ypeer(k))
    def word_send(r):
        for k in (1, NZ - 1):
            pl.semaphore_signal(word.at[r], inc=1, device_id=zpeer(k), device_id_type=MESH)

    word_send(0)
    lo.wait()
    lp.wait()
    lk.wait()
    lf.wait()
    place = posq[z].astype(F32)
    angles = jnp.broadcast_to(place, (TOK, HEAD_DIM)).T * freq_v[...]
    cosine, sine = jnp.cos(angles), jnp.sin(angles)

    la.wait()

    def acts(owner):
        return act_v[:, pl.ds(pl.multiple_of(owner * 1024, 1024), 1024)]

    proj[...] = nn(acts(y), w_v[rows(y, 1024), :])
    def along_x(blk, sem_x, sem_c):
        for k in (2, 1, 3):
            send(blk, blk, sem_x.at[k - 1], xpeer(k))
        send(blk, blk, sem_c.at[0], sibling)

    pl.semaphore_wait(word.at[0], 2)
    word_send(1)
    for k in YORDER:
        wshare(Q, k)
    pl.semaphore_wait(word.at[1], 2)
    word_send(2)
    wshare(K, 1)
    wshare(K, 3)
    pl.semaphore_wait(word.at[2], 2)
    for k in range(1, NZ):
        blk = posq.at[z]
        send(blk, blk, psem, zpeer(k))
    for k, d in cross:
        blk = posk.at[xc]
        dev = device(lax.rem(x + k, NX), y, z, c if d == 0 else other)
        send(blk, blk, ksem, dev)
    for k in range(1, NZ):
        blk = og_all.at[rows(z, TOK)]
        send(blk, blk, osem, zpeer(k))
    wpass(Q, 1)
    wpass(Q, 3)
    wshare(V, 1)
    wshare(V, 3)
    wpass(Q, 2)
    wshare(K, 2)
    for k in YORDER:
        wuse(Q, k)
    queries = proj[:, third(Q)]
    queries = queries * cosine + turn(queries) * sine
    q_all[rows(z, TOK), :] = queries.astype(BF)
    for k in (4, 3, 5, 2, 6, 1, 7):
        blk = q_all.at[rows(z, TOK)]
        send(blk, blk, qsem, zpeer(k))
    wshare(V, 2)
    for k in YORDER:
        wpass(K, k)
    wpass(V, 1)
    wpass(V, 3)
    for k in YORDER:
        wuse(K, k)
    keys = proj[:, third(K)]
    keys = keys * cosine + turn(keys) * sine
    k_all[xc] = keys.astype(BF)
    along_x(k_all.at[xc], kxsem, kcsem)
    wpass(V, 2)
    for k in YORDER:
        wuse(V, k)
    v_all[xc] = proj[:, third(V)].astype(BF)
    along_x(v_all.at[xc], vxsem, vcsem)

    for k, d in cross:
        to_y, to_c = lax.rem(y + k, NY), c if d == 0 else other
        src = act_v.at[:, pl.ds(pl.multiple_of(to_y * 1024 + to_c * 512, 512), 512)]
        send(src, actx.at[yc], asem, device(x, to_y, z, to_c))
    lx = pltpu.make_async_copy(
        act_v.at[:, pl.ds(pl.multiple_of(y * 1024 + c * 512, 512), 512)], actx.at[yc], lsem.at[3]
    )
    lx.start()

    arrived(posq.at[pl.ds(0, 7)], psem)
    arrived(posk.at[pl.ds(0, 7)], ksem)
    for kb in range(8):
        poskt[kb] = jnp.broadcast_to(posk[kb].astype(F32), (TOK, TOK)).T
    place_q = jnp.concatenate([posq[i].astype(F32) for i in range(NZ)], 1)
    arrived(og_all.at[pl.ds(0, 7 * TOK)], osem)

    def block_of(step):
        dx, dc = STEPS[step]
        return lax.rem(x - dx + NX, NX) * 2 + (c if dc == 0 else other)

    def relay(buf, sem_x, sem_c):
        for k in (1, 3, 2):
            blk = buf.at[lax.rem(x - k + NX, NX) * 2 + c]
            arrived(blk, sem_x.at[k - 1])
            send(blk, blk, sem_c.at[k], sibling)

    relay(k_all, kxsem, kcsem)
    relay(v_all, vxsem, vcsem)
    arrived(q_all.at[pl.ds(0, 7 * TOK)], qsem)

    def first(step, half):
        kb = block_of(step)
        dx, dc = STEPS[step]
        if half == 0:
            if dc:
                arrived(k_all.at[kb], kcsem.at[dx])
                arrived(v_all.at[kb], vcsem.at[dx])
            kt_all[kb] = k_all[kb].T
        pk = poskt[kb]
        pk = jnp.concatenate([pk, pk], 1)
        for j in (2 * half, 2 * half + 1):
            cols = pl.ds(j * 256, 256)
            s = nt(k_all[kb], q_all[cols, :])
            dp = nt(v_all[kb], og_all[cols, :])
            s = jnp.where(place_q[:, j * 256 : (j + 1) * 256] >= pk, s, LOW)
            top = jnp.max(s, 0, keepdims=True)
            e = jnp.exp2((s - top) * EXP2_SCALE)
            e_all[kb, :, cols] = e
            dp_all[kb, :, cols] = dp
            mb[pl.ds(kb, 1), cols] = top
            lb[pl.ds(kb, 1), cols] = jnp.sum(e, 0, keepdims=True)
            ab[pl.ds(kb, 1), cols] = jnp.sum(e * dp, 0, keepdims=True)

    def stats_send(half):
        cols = pl.ds(half * 512, 512)
        high = mb[:, cols]
        top = jnp.max(high, 0, keepdims=True)
        fade = jnp.exp2((high - top) * EXP2_SCALE)
        total = jnp.sum(lb[:, cols] * fade, 0, keepdims=True)
        st_all[half, z, 0:1, :] = top * EXP2_SCALE + jnp.log2(total)
        st_all[half, z, 1:2, :] = jnp.sum(ab[:, cols] * fade, 0, keepdims=True) / total
        blk = st_all.at[half, z]
        for k in (4, 3, 5, 2, 6, 1, 7):
            send(blk, blk, ssem.at[half], zpeer(k))

    def stats_merge(half):
        cols = pl.ds(half * 512, 512)
        arrived(st_all.at[half, pl.ds(0, 7)], ssem.at[half])
        top = st_all[half, 0, 0:1, :]
        for i in range(1, NZ):
            top = jnp.maximum(top, st_all[half, i, 0:1, :])
        total = jnp.zeros((1, 512), F32)
        delta = jnp.zeros((1, 512), F32)
        for i in range(NZ):
            fade = jnp.exp2(st_all[half, i, 0:1, :] - top)
            total += fade
            delta += st_all[half, i, 1:2, :] * fade
        dl[:, cols] = delta / total
        mb[:, cols] = jnp.exp2(mb[:, cols] * EXP2_SCALE - (top + jnp.log2(total)))

    def grads_of(kb, j):
        cols = pl.ds(j * 256, 256)
        p = e_all[kb, :, cols] * mb[pl.ds(kb, 1), cols]
        ds = (p * (dp_all[kb, :, cols] - dl[:, cols])).astype(BF)
        ds_all[rows(kb, TOK), cols] = ds
        return p.astype(BF), ds

    def dq_send(half):
        kt = jnp.concatenate([kt_all[i] for i in range(8)], 1)
        for j in (2 * half, 2 * half + 1):
            dq = nn(kt, ds_all[:, j * 256 : (j + 1) * 256]) * SCALE
            dq_out[2 * j] = dq[:, :TOK].astype(BF)
            dq_out[2 * j + 1] = dq[:, TOK:].astype(BF)
        for k in (4, 3, 5, 2, 6, 1, 7):
            to = lax.rem(z + k, NZ)

            @pl.when(to // 4 == half)
            def _():
                pltpu.make_async_remote_copy(
                    dq_out.at[to], dq_in.at[z], sent, dqsem,
                    device_id=zpeer(k), device_id_type=MESH,
                ).start()

    for step in range(8):
        first(step, 0)
    stats_send(0)
    for step in range(8):
        first(step, 1)
    stats_send(1)
    stats_merge(0)

    for kb in range(8):
        dv = jnp.zeros((TOK, HEAD_DIM), F32)
        dk = jnp.zeros((TOK, HEAD_DIM), F32)
        for j in range(2):
            cols = pl.ds(j * 256, 256)
            p, ds = grads_of(kb, j)
            dv += nn(p, og_all[cols, :])
            dk += nn(ds, q_all[cols, :])
        acc_k[kb] = dk
        acc_v[kb] = dv
    dq_send(0)
    stats_merge(1)
    for kb in range(8):
        for j in range(2, 4):
            p, ds = grads_of(kb, j)
            p_all[kb, :, pl.ds((j - 2) * 256, 256)] = p
    dq_send(1)

    XORDER = (2, 1, 3, 0)

    def value_grad(kb):
        return acc_v[kb] + nn(p_all[kb], og_all[512:, :])

    def key_grad(kb):
        return (acc_k[kb] + nn(ds_all[rows(kb, TOK), 512:], q_all[512:, :])) * SCALE

    def to_sibling(i, grad):
        for k in XORDER:
            dc_out[i, k] = grad(lax.rem(x + k, NX) * 2 + other).astype(BF)
        send(dc_out.at[i], dc_in.at[i], dcsem.at[i], sibling)

    def to_owners(i, own):
        arrived(dc_in.at[i], dcsem.at[i])
        for k in XORDER:
            dx_out[i, k] = (own[k] + dc_in[i, k].astype(F32)).astype(BF)
        for k in XORDER[:3]:
            send(dx_out.at[i, k], dx_in.at[i, k], dxsem.at[i], xpeer(k))

    def collect(i):
        arrived(dx_in.at[i, pl.ds(1, 3)], dxsem.at[i])
        total = dx_out[i, 0].astype(F32)
        for k in range(1, NX):
            total += dx_in[i, k].astype(F32)
        return total

    to_sibling(0, value_grad)
    to_sibling(1, key_grad)
    for k in XORDER:
        acc_own[0, k] = value_grad(lax.rem(x + k, NX) * 2 + c)
    for k in XORDER:
        acc_own[1, k] = key_grad(lax.rem(x + k, NX) * 2 + c)
    to_owners(0, acc_own.at[0])
    to_owners(1, acc_own.at[1])
    lx.wait()
    arrived(actx.at[pl.ds(0, 7)], asem)

    def turn_block(b, carry):
        actxt[:, pl.ds(pl.multiple_of(b * TOK, TOK), TOK)] = actx[b].T
        return carry

    lax.fori_loop(0, 8, turn_block, 0)
    def gp_send(i):
        blk = gp_all.at[yc, :, third(i)]
        for k in (2, 1, 3):
            send(blk, blk, gsem_y.at[i, k - 1], ypeer(k))
        send(blk, blk, gsem_c.at[i], sibling)

    def gp_relay(i):
        for k in YORDER:
            blk = gp_all.at[lax.rem(y - k + NY, NY) * 2 + c, :, third(i)]
            arrived(blk, gsem_y.at[i, k - 1])
            send(blk, blk, gsem_c.at[i], sibling)

    def dw_send(i):
        arrived(gp_all.at[pl.ds(0, 4), :, third(i)], gsem_c.at[i])
        gp = gp_all[:, :, third(i)].reshape(8 * TOK, HEAD_DIM)
        for j in range(NX):
            dwx_out[i, j] = nn(actxt[j * 128 : (j + 1) * 128, :], gp).astype(BF)
        for k in (2, 1, 3):
            to = lax.rem(x + k, NX)
            send(dwx_out.at[i, to], dwx_in.at[i, x], xsem.at[i], xpeer(k))

    def band_send(i):
        arrived(dwx_in.at[i, pl.ds(0, 3)], xsem.at[i])
        dw = dwx_out[i, x].astype(F32)
        for k in range(1, NX):
            dw += dwx_in[i, lax.rem(x + k, NX)].astype(F32)
        dwz_out[i] = dw.astype(BF).reshape(8, 16, HEAD_DIM)
        for k in (4, 3, 5, 2, 6, 1, 7):
            to = lax.rem(z + k, NZ)
            send(dwz_out.at[i, to], dwz_in.at[i, z], zsem.at[i], zpeer(k))

    def band(i, xx, cc):
        return dw_all.at[i, pl.ds(pl.multiple_of(cc * 512 + xx * 128, 128), 128)]

    def piece_send(i):
        arrived(dwz_in.at[i, pl.ds(0, 7)], zsem.at[i])
        dw = dwz_out[i, z].astype(F32)
        for k in range(1, NZ):
            dw += dwz_in[i, lax.rem(z + k, NZ)].astype(F32)
        own = pl.ds(pl.multiple_of(c * 512 + x * 128 + z * 16, 16), 16)
        dw_all[i, own, :] = dw.astype(BF)
        blk = dw_all.at[i, own]
        for k in (4, 3, 5, 2, 6, 1, 7):
            send(blk, blk, zgsem.at[i], zpeer(k))

    def spread(i):
        arrived(dw_all.at[i, pl.ds(0, 7 * 16)], zgsem.at[i])
        blk = band(i, x, c)
        for k in (2, 1, 3):
            send(blk, blk, xgsem.at[i, k - 1], xpeer(k))
        send(blk, blk, sgsem.at[i], sibling)

    def spread_relay(i):
        for k in (1, 3, 2):
            blk = band(i, lax.rem(x - k + NX, NX), c)
            arrived(blk, xgsem.at[i, k - 1])
            send(blk, blk, sgsem.at[i], sibling)

    def finish(i):
        arrived(dw_all.at[i, pl.ds(0, 512)], sgsem.at[i])
        gw_ref[:, third(i)] = dw_all[i].astype(F32)

    gp_all[yc, :, third(2)] = collect(0).astype(BF)
    gp_send(2)
    dkey = collect(1)
    dkey = dkey * cosine - turn(dkey) * sine
    gp_all[yc, :, third(1)] = dkey.astype(BF)
    gp_send(1)
    arrived(dq_in.at[pl.ds(0, 7)], dqsem)
    dq = dq_out[z].astype(F32)
    for k in range(1, NZ):
        dq += dq_in[lax.rem(z + k, NZ)].astype(F32)
    dq = dq.T
    dq = dq * cosine - turn(dq) * sine
    gp_all[yc, :, :HEAD_DIM] = dq.astype(BF)
    gp_send(0)

    def acts_grad(j, carry):
        cols = pl.ds(pl.multiple_of(j * 512, 512), 512)
        ga_ref[0, :, cols] = nt(gp_all[yc], w_v[cols, :])
        return carry

    lax.fori_loop(0, 3, acts_grad, 0)
    gp_relay(2)
    lax.fori_loop(3, 5, acts_grad, 0)
    gp_relay(1)
    dw_send(2)
    gp_relay(0)
    dw_send(1)
    dw_send(0)
    band_send(2)
    band_send(1)
    band_send(0)
    piece_send(2)
    lax.fori_loop(5, 8, acts_grad, 0)
    piece_send(1)
    piece_send(0)
    spread(2)
    spread(1)
    spread(0)
    spread_relay(2)
    spread_relay(1)
    finish(2)
    spread_relay(0)
    finish(1)
    finish(0)

    blk = dq_out.at[pl.ds(0, 7)]
    pltpu.make_async_remote_copy(
        blk, blk, sent, dqsem, device_id=sibling, device_id_type=MESH
    ).wait_send()
    for cp in sends:
        cp.wait_send()


def put(ga_ref, gw_ref, ga_hbm, gw_hbm, sem):
    copies = []
    for i in range(2):
        part = pl.ds(i * 64, 64)
        copies.append(pltpu.make_async_copy(ga_ref.at[0, part], ga_hbm.at[0, part], sem.at[0, i]))
        part = pl.ds(i * 512, 512)
        copies.append(pltpu.make_async_copy(gw_ref.at[part], gw_hbm.at[part], sem.at[1, i]))
    for cp in copies:
        cp.start()
    for cp in copies:
        cp.wait()


def shards(activations, weights, positions, out_grad):
    steps = np.arange(HEAD_DIM // 2, dtype=np.float64)
    freq = (ROPE_BASE ** (-(steps * 2.0 / HEAD_DIM))).astype(np.float32)
    freq = jnp.asarray(np.concatenate([freq, freq])[None])
    operands = (freq, activations, weights, positions, out_grad)
    hbm = pl.BlockSpec(memory_space=pltpu.HBM)
    vmem = pl.BlockSpec(memory_space=pltpu.VMEM)
    dma = pltpu.SemaphoreType.DMA
    V = pltpu.VMEM
    scratch = [
        V((1, HEAD_DIM), F32), V((TOK, 4096), BF), V((4096, WIDE), BF), V((1024, HEAD_DIM), BF), V((1024, HEAD_DIM), BF),
        V((NZ, 1, TOK), jnp.int32), V((8, 1, TOK), jnp.int32), V((8, TOK, TOK), F32),
        V((8, TOK, HEAD_DIM), BF), V((8, TOK, HEAD_DIM), BF), V((8, HEAD_DIM, TOK), BF), V((TOK, WIDE), F32),
        V((8, TOK, 1024), F32), V((8, TOK, 1024), F32), V((1024, 1024), BF),
        V((8, 1024), F32), V((8, 1024), F32), V((8, 1024), F32), V((1, 1024), F32),
        V((8, TOK, HEAD_DIM), F32), V((8, TOK, HEAD_DIM), F32), V((8, TOK, 512), BF), V((2, NZ, 2, 512), F32),
        V((NZ, HEAD_DIM, TOK), BF), V((NZ, HEAD_DIM, TOK), BF),
        V((2, NX, TOK, HEAD_DIM), F32), V((2, NX, TOK, HEAD_DIM), BF), V((2, NX, TOK, HEAD_DIM), BF),
        V((2, NX, TOK, HEAD_DIM), BF), V((2, NX, TOK, HEAD_DIM), BF),
        V((8, TOK, WIDE), BF), V((8, TOK, 512), BF), V((512, 1024), BF),
        V((3, NX, 128, 128), BF), V((3, NX, 128, 128), BF), V((8, 128), F32),
        V((3, NZ, 16, 128), BF), V((3, NZ, 16, 128), BF), V((3, 1024, 128), BF),
        pltpu.SemaphoreType.REGULAR((3,)), dma(()), dma((4,)), dma((3, 3)), dma((3, 3)), dma((3, 3)), dma(()), dma(()), dma(()), dma(()),
        dma((3,)), dma((4,)), dma((3,)), dma((4,)), dma(()), dma((2,)), dma(()), dma((2,)), dma((2,)), dma((3, 3)), dma((3,)), dma((3,)),
        dma((3,)), dma((3,)), dma((3, 3)), dma((3,)),
    ]
    grads = pl.pallas_call(
        kernel,
        out_shape=(pltpu.VMEM((1, TOK, 4096), F32), pltpu.VMEM((1024, WIDE), F32)),
        in_specs=[hbm] * 5,
        out_specs=(vmem, vmem),
        scratch_shapes=scratch,
        compiler_params=pltpu.CompilerParams(
            collective_id=0, has_side_effects=True, vmem_limit_bytes=40 << 20
        ),
    )(*(pltpu.with_memory_space_constraint(a, pltpu.HBM) for a in operands))
    return pl.pallas_call(
        put,
        out_shape=(
            jax.ShapeDtypeStruct((1, TOK, 4096), F32),
            jax.ShapeDtypeStruct((1024, WIDE), F32),
        ),
        in_specs=[vmem, vmem],
        out_specs=(hbm, hbm),
        scratch_shapes=[dma((2, 2))],
        compiler_params=pltpu.CompilerParams(vmem_limit_bytes=8 << 20),
    )(*grads)


def solution(mesh):
    placed = (
        P("dp", ("outer", "inner"), None),
        P("dp", None),
        P("dp", ("outer", "inner")),
        P("dp", ("outer", "inner"), None),
    )
    return jax.shard_map(
        shards,
        mesh=mesh,
        in_specs=placed,
        out_specs=(P("dp", ("outer", "inner"), None), P("dp", None)),
        check_vma=False,
    )
```
